256 devices in a mesh: dp: 4 (over x_lo, core), space: 64 (over y, z, x_hi).
Axes of the slice: x: 4 (x_hi: 2, x_lo: 2; x = x_hi * 2 + x_lo), y: 4, z: 8, core: 2. Of those that a mesh axis runs over, the one named last changes fastest.
Arguments:
- volume: bfloat16 [4, 512, 32, 2048], P('dp', 'space'), may hold values from -6 to 6
- weight_first: bfloat16 [1728, 128], P('dp'), may hold values from -0.15625 to 0.15625
- weight_second: bfloat16 [3456, 256], P('dp'), may hold values from -0.109375 to 0.109375
- cotangent: bfloat16 [4, 128, 8, 2048], P('dp', 'space'), may hold values from -16 to 16
Outputs:
- activations: bfloat16 [4, 128, 8, 2048], P('dp', 'space')
- input_gradient: bfloat16 [4, 512, 32, 2048], P('dp', 'space')
- first_gradient: float32 [1728, 128], P('dp')
- second_gradient: float32 [3456, 256], P('dp')
The draws below stay inside these ranges and needn't reach their ends.
All inputs are finite; a program needn't handle non-finite values.
Results may differ from the reference program's by a relative error of at most 0.012.
Values may be sent and summed in bfloat16 or wider, within the bound.
A program may use at most 64 MiB of HBM per device.

```python
import jax
import jax.numpy as jnp
from jax import lax

CIN = 64
CMID = 128
COUT = 256
S = 32
BATCH = 4
NX = 512


def with_spikes(values, stream_key, source, target, shards_of, factor):
    def block_of(axis_at):
        return (jnp.arange(values.shape[axis_at]) // (values.shape[axis_at] // shards_of)).reshape((-1,) + (1,) * (values.ndim - 1 - axis_at))

    first = jax.random.permutation(stream_key, shards_of)[block_of(target)]
    far = (block_of(target) + shards_of // 2) % shards_of
    return jnp.where((block_of(source) == first) | (block_of(source) == far), factor * values, values)


def steps_of(rng, extent, split, least, largest):
    factor_of, own = 1.0, jax.random.fold_in(rng, 6)
    for position, parts in split:
        heights = jnp.exp(jax.random.uniform(jax.random.fold_in(own, position), (parts,), jnp.float32, least / len(split), largest / len(split)))
        factor_of = factor_of * jnp.repeat(heights, extent[position] // parts).reshape([-1 if axis == position else 1 for axis in range(len(extent))])
    return factor_of


def scatter_about(stream_key, extent, spread, bound, shards=(), dtype=jnp.bfloat16):
    drawn = spread * jax.random.normal(stream_key, extent, jnp.float32)
    if shards:
        drawn = drawn * steps_of(stream_key, extent, shards, -0.22, 0.18)
    return jnp.clip(drawn, -bound, bound).astype(dtype)


def noise_with(rng, shape, scale, limit, split, heavy, kind=jnp.bfloat16):
    drawn = scale * jax.random.normal(rng, shape, jnp.float32)
    if split:
        drawn = drawn * steps_of(rng, shape, split, -0.22, 0.18)
    return jnp.clip(with_spikes(drawn, jax.random.fold_in(rng, 3), *heavy), -limit, limit).astype(kind)


def setup_inputs(seed: int = 0) -> dict:
    keys = jax.random.split(jax.random.key(seed), 5)
    volume = scatter_about(keys[0], (BATCH, NX, S, S * CIN), 1.0, 6.0, ((0, 4), (1, 64)))
    weight_first = scatter_about(keys[1], (27 * CIN, CMID), (27 * CIN) ** -0.5, 0.15625, ((0, 4),))
    weight_second = scatter_about(keys[2], (27 * CMID, COUT), (27 * CMID) ** -0.5, 0.109375, ((0, 4),))
    cotangent = noise_with(keys[3], (BATCH, NX // 4, S // 4, (S // 4) * COUT), 1.0, 16.0, ((0, 4), (1, 64)), (1, 3, 64, 4.0))
    return dict(volume=volume, weight_first=weight_first, weight_second=weight_second, cotangent=cotangent)


LEAK_SLOPE = 0.2
LAYOUT = ("NDHWC", "DHWIO", "NDHWC")


def activate(values):
    return LEAK_SLOPE * values + (1.0 - LEAK_SLOPE) * jax.nn.softplus(values)


def activate_slope(values):
    return LEAK_SLOPE + (1.0 - LEAK_SLOPE) * jax.nn.sigmoid(values)


def pad_lower(tensor):
    return jnp.pad(tensor, ((0, 0), (1, 0), (1, 0), (1, 0), (0, 0)))


def convolve(padded, kernel):
    return lax.conv_general_dilated(padded, kernel, (2, 2, 2), ((0, 0), (0, 0), (0, 0)), dimension_numbers=LAYOUT, preferred_element_type=jnp.float32)


def convolve_back(delta, kernel):
    flipped = jnp.transpose(kernel[::-1, ::-1, ::-1], (0, 1, 2, 4, 3))
    return lax.conv_general_dilated(delta, flipped, (1, 1, 1), ((2, 2), (1, 2), (1, 2)), lhs_dilation=(2, 2, 2), dimension_numbers=LAYOUT, preferred_element_type=jnp.float32)


def kernel_gradient(padded, delta):
    samples, out_depth, out_rows, out_columns, features = delta.shape
    channels = padded.shape[-1]
    flat_delta = delta.reshape(-1, features)
    pieces = []
    for offset in range(27):
        depth_tap = offset // 9
        row_tap = offset // 3 % 3
        column_tap = offset % 3
        window = lax.slice(padded, (0, depth_tap, row_tap, column_tap, 0), (samples, depth_tap + 2 * out_depth - 1, row_tap + 2 * out_rows - 1, column_tap + 2 * out_columns - 1, channels), (1, 2, 2, 2, 1))
        pieces.append(jnp.dot(window.reshape(-1, channels).T, flat_delta, preferred_element_type=jnp.float32))
    return jnp.concatenate(pieces, axis=0)


def reference(volume, weight_first, weight_second, cotangent):
    samples = volume.shape[0]
    depth_cells = volume.shape[1]
    side_cells = volume.shape[2]
    kernel_first = weight_first.reshape(3, 3, 3, CIN, CMID)
    kernel_second = weight_second.reshape(3, 3, 3, CMID, COUT)

    def sample_pass(operands):
        sample_volume, sample_cot = operands
        inputs = sample_volume.reshape(1, depth_cells, side_cells, side_cells, CIN)
        padded_input = pad_lower(inputs)
        linear_first = convolve(padded_input, kernel_first)
        hidden = activate(linear_first).astype(jnp.bfloat16)
        padded_hidden = pad_lower(hidden)
        linear_second = convolve(padded_hidden, kernel_second)
        activations = activate(linear_second).astype(jnp.bfloat16)
        incoming = sample_cot.reshape(linear_second.shape).astype(jnp.float32)
        delta_second = (incoming * activate_slope(linear_second)).astype(jnp.bfloat16)
        hidden_delta = convolve_back(delta_second, kernel_second)[:, 1:]
        delta_first = (hidden_delta * activate_slope(linear_first)).astype(jnp.bfloat16)
        input_delta = convolve_back(delta_first, kernel_first)[:, 1:].astype(jnp.bfloat16)
        return (activations.reshape(sample_cot.shape), input_delta.reshape(sample_volume.shape), kernel_gradient(padded_input, delta_first), kernel_gradient(padded_hidden, delta_second))

    activations, input_gradient, tally_first, tally_second = lax.map(sample_pass, (volume, cotangent))
    cells_first = samples * (depth_cells // 2) * (side_cells // 2) * (side_cells // 2)
    cells_second = samples * (depth_cells // 4) * (side_cells // 4) * (side_cells // 4)
    first_gradient = jnp.sum(tally_first, axis=0) * (float(cells_first) ** -0.5)
    second_gradient = jnp.sum(tally_second, axis=0) * (float(cells_second) ** -0.5)
    return activations, input_gradient, first_gradient, second_gradient
```

```python
import functools

import jax
import jax.numpy as jnp
from jax import lax
from jax.experimental import pallas as pl
from jax.experimental.pallas import tpu as pltpu
from jax.sharding import PartitionSpec as P

CIN = 64
CMID = 128
COUT = 256


LEAK_SLOPE = 0.2
LAYOUT = ("NDHWC", "DHWIO", "NDHWC")
NY, NZ = 4, 8
PIECE = 80
BF, F32 = jnp.bfloat16, jnp.float32


def shifted(x, axis, by):
    length = lax.axis_size(axis)
    pairs = [(i, i + by) for i in range(length) if 0 <= i + by < length]
    return lax.ppermute(x, axis, pairs)


def activate(values):
    return LEAK_SLOPE * values + (1.0 - LEAK_SLOPE) * jax.nn.softplus(values)


def activate_slope(values):
    return LEAK_SLOPE + (1.0 - LEAK_SLOPE) * jax.nn.sigmoid(values)


def pad_sides(tensor):
    return jnp.pad(tensor, ((0, 0), (0, 0), (1, 0), (1, 0), (0, 0)))


def convolve(padded, kernel):
    return lax.conv_general_dilated(
        padded,
        kernel,
        (2, 2, 2),
        ((0, 0), (0, 0), (0, 0)),
        dimension_numbers=LAYOUT,
        preferred_element_type=jnp.float32,
    )


def convolve_back(delta, kernel):
    flipped = jnp.transpose(kernel[::-1, ::-1, ::-1], (0, 1, 2, 4, 3))
    return lax.conv_general_dilated(
        delta,
        flipped,
        (1, 1, 1),
        ((2, 2), (1, 2), (1, 2)),
        lhs_dilation=(2, 2, 2),
        dimension_numbers=LAYOUT,
        preferred_element_type=jnp.float32,
    )


def kernel_gradient(padded, delta):
    channels = padded.shape[-1]
    features = delta.shape[-1]
    tapped = lax.conv_general_dilated(
        padded,
        delta,
        (1, 1, 1),
        ((0, 0), (0, 0), (0, 0)),
        rhs_dilation=(2, 2, 2),
        dimension_numbers=("CDHWN", "IDHWO", "NDHWC"),
        preferred_element_type=jnp.float32,
    )
    return jnp.transpose(tapped, (1, 2, 3, 0, 4)).reshape(27 * channels, features)


def place():
    d, s = lax.axis_index("dp"), lax.axis_index("space")
    return d // 2, d % 2, s // 16, (s // 2) % NZ, s % 2


def device(xl, core, y, z, xh):
    return {"dp": xl * 2 + core, "space": (y * NZ + z) * 2 + xh}


def remote(src, dst, send, recv, target):
    return pltpu.make_async_remote_copy(
        src_ref=src,
        dst_ref=dst,
        send_sem=send,
        recv_sem=recv,
        device_id=target,
        device_id_type=pl.DeviceIdType.MESH,
    )


def reduce_kernel(s_ref, out_ref, r1, hy, r2, hz, r3, kx, r4, g, s1, q1, s2, q2, s3, q3, s4, q4, s5, q5, s6, q6):
    xl, core, y, z, xh = place()

    barrier = pltpu.get_barrier_semaphore()
    peers = [device(xl, 1 - core, y, z, xh)]
    peers += [device(xl, core, (y + k) % NY, z, xh) for k in range(1, NY)]
    peers += [device(xl, core, y, (z + k) % NZ, xh) for k in range(1, NZ)]
    peers += [device(1 - xl, core, y, z, xh), device(xl, core, y, z, 1 - xh), device(1 - xl, core, y, z, 1 - xh)]
    for peer in peers:
        pl.semaphore_signal(barrier, inc=1, device_id=peer, device_id_type=pl.DeviceIdType.MESH)
    pl.semaphore_wait(barrier, len(peers))

    order = (1, 3, 2, 0)
    first = {}
    for k in order:
        there = (y + k) % NY
        for h in range(2):
            first[k, h] = remote(s_ref.at[h * 2 + 1 - core, there], r1.at[k, h], s1.at[k, h], q1.at[k, h], peers[0])
            first[k, h].start()
    second = {}
    for k in order:
        there = (y + k) % NY
        for h in range(2):
            first[k, h].wait_recv()

            @pl.loop(0, NZ)
            def _(i, h=h, k=k, there=there):
                hy[k, h, i] = (s_ref[h * 2 + core, there, i].astype(F32) + r1[k, h, i].astype(F32)).astype(BF)

        if k:
            second[k] = remote(hy.at[k], r2.at[k - 1], s2.at[k - 1], q2.at[k - 1], peers[k])
            second[k].start()
    for k in range(1, NY):
        second[k].wait_recv()
    third = {}
    for k in (4, 3, 5, 2, 6, 1, 7, 0):
        there = (z + k) % NZ
        for h in range(2):
            total = hy[0, h, there].astype(F32)
            for j in range(NY - 1):
                total += r2[j, h, there].astype(F32)
            hz[k, h] = total.astype(BF)
        if k:
            third[k] = remote(hz.at[k], r3.at[k - 1], s3.at[k - 1], q3.at[k - 1], peers[3 + k])
            third[k].start()
    for k in range(1, NZ):
        third[k].wait_recv()
    for h in range(2):
        total = hz[0, h].astype(F32)
        for j in range(NZ - 1):
            total += r3[j, h].astype(F32)
        kx[h] = total.astype(BF)
    fourth = []
    for j, half in enumerate((1 - xl, xl, 1 - xl)):
        fourth.append(remote(kx.at[half], r4.at[j], s4.at[j], q4.at[j], peers[11 + j]))
        fourth[j].start()
    total = kx[xl].astype(F32)
    for j in range(3):
        fourth[j].wait_recv()
        total += r4[j].astype(F32)
    g[y, z] = total.astype(BF)
    fifth = {}
    for k in (4, 3, 5, 2, 6, 1, 7):
        fifth[k] = remote(g.at[y, z], g.at[y, z], s5.at[k - 1], q5.at[k - 1], peers[3 + k])
        fifth[k].start()
    for k in range(1, NZ):
        fifth[k].wait_recv()
    sixth = {}
    for k in (2, 1, 3):
        sixth[k] = remote(g.at[y], g.at[y], s6.at[k - 1], q6.at[k - 1], peers[k])
        sixth[k].start()
    for k in range(1, NY):
        sixth[k].wait_recv()

    @pl.loop(0, NY)
    def _(i):
        @pl.loop(0, NZ)
        def _(j):
            out_ref[i, j] = g[i, j].astype(F32)

    for copies in (first, second, third, dict(enumerate(fourth)), fifth, sixth):
        for copy in copies.values():
            copy.wait_send()


def reduce_gradients(sums):
    dma = pltpu.SemaphoreType.DMA
    return pl.pallas_call(
        reduce_kernel,
        out_shape=jax.ShapeDtypeStruct((NY, NZ, PIECE, 128), F32),
        in_specs=[pl.BlockSpec(memory_space=pltpu.VMEM)],
        out_specs=pl.BlockSpec(memory_space=pltpu.VMEM),
        scratch_shapes=[
            pltpu.VMEM((NY, 2, NZ, PIECE, 128), BF),
            pltpu.VMEM((NY, 2, NZ, PIECE, 128), BF),
            pltpu.VMEM((NY - 1, 2, NZ, PIECE, 128), BF),
            pltpu.VMEM((NZ, 2, PIECE, 128), BF),
            pltpu.VMEM((NZ - 1, 2, PIECE, 128), BF),
            pltpu.VMEM((2, PIECE, 128), BF),
            pltpu.VMEM((3, PIECE, 128), BF),
            pltpu.VMEM((NY, NZ, PIECE, 128), BF),
            dma((NY, 2)), dma((NY, 2)),
            dma((NY - 1,)), dma((NY - 1,)),
            dma((NZ - 1,)), dma((NZ - 1,)),
            dma((3,)), dma((3,)),
            dma((NZ - 1,)), dma((NZ - 1,)),
            dma((NY - 1,)), dma((NY - 1,)),
        ],
        compiler_params=pltpu.CompilerParams(collective_id=0, has_side_effects=True),
        name="reduce_gradients",
    )(sums)


def local(volume, weight_first, weight_second, cotangent):
    samples = volume.shape[0]
    planes = volume.shape[1]
    side_cells = volume.shape[2]
    kernel_first = lax.all_gather(weight_first, "dp", axis=0, tiled=True).reshape(
        3, 3, 3, CIN, CMID
    )
    kernel_second = lax.all_gather(weight_second, "dp", axis=0, tiled=True).reshape(
        3, 3, 3, CMID, COUT
    )
    inputs = volume.reshape(samples, planes, side_cells, side_cells, CIN)
    lower_input = shifted(inputs[:, planes - 1 :], "space", 1)
    padded_input = pad_sides(jnp.concatenate([lower_input, inputs], axis=1))
    linear_first = convolve(padded_input, kernel_first)
    hidden = activate(linear_first).astype(jnp.bfloat16)
    half_planes = hidden.shape[1]
    lower_hidden = shifted(hidden[:, half_planes - 1 :], "space", 1)
    padded_hidden = pad_sides(jnp.concatenate([lower_hidden, hidden], axis=1))
    linear_second = convolve(padded_hidden, kernel_second)
    activations = activate(linear_second).astype(jnp.bfloat16)
    incoming = cotangent.reshape(linear_second.shape).astype(jnp.float32)
    delta_second = (incoming * activate_slope(linear_second)).astype(jnp.bfloat16)
    spread = convolve_back(delta_second, kernel_second)
    upper_rim = shifted(spread[:, :1].astype(jnp.bfloat16), "space", -1).astype(jnp.float32)
    hidden_delta = jnp.concatenate([spread[:, 1:-1], spread[:, -1:] + upper_rim], axis=1)
    delta_first = (hidden_delta * activate_slope(linear_first)).astype(jnp.bfloat16)
    spread_input = convolve_back(delta_first, kernel_first)
    upper_input = shifted(spread_input[:, :1].astype(jnp.bfloat16), "space", -1).astype(jnp.float32)
    input_delta = jnp.concatenate(
        [spread_input[:, 1:-1], spread_input[:, -1:] + upper_input], axis=1
    )
    input_gradient = input_delta.astype(jnp.bfloat16)
    tally_first = kernel_gradient(padded_input, delta_first).astype(BF).reshape(4, 432, 128)
    tally_second = kernel_gradient(padded_hidden, delta_second).astype(BF).reshape(4, 864, 256)
    sums = jnp.concatenate(
        [tally_first, tally_second[..., :128], tally_second[..., 128:], jnp.zeros((4, 400, 128), BF)], axis=1
    ).reshape(4, NY, NZ, PIECE, 128)
    total = reduce_gradients(sums).reshape(NY * NZ * PIECE, 128)
    first_gradient = total[:432] * 262144.0**-0.5
    second_gradient = jnp.concatenate([total[432:1296], total[1296:2160]], axis=1) * 32768.0**-0.5
    return (
        activations.reshape(cotangent.shape),
        input_gradient.reshape(volume.shape),
        first_gradient,
        second_gradient,
    )


def solution(mesh):
    return jax.shard_map(
        local,
        mesh=mesh,
        in_specs=(
            P("dp", "space", None, None),
            P("dp", None),
            P("dp", None),
            P("dp", "space", None, None),
        ),
        out_specs=(
            P("dp", "space", None, None),
            P("dp", "space", None, None),
            P("dp", None),
            P("dp", None),
        ),
        check_vma=False,
    )
```

```python
import numpy as np

import jax
import jax.numpy as jnp
from jax import lax
from jax.experimental import pallas as pl
from jax.experimental.pallas import tpu as pltpu
from jax.sharding import PartitionSpec as P

NY, NZ = 4, 8
BF, F32 = jnp.bfloat16, jnp.float32
R1ROWS, R2ROWS = 512, 2048
MESH = pl.DeviceIdType.MESH


def rank_of(p):
    return (p % 2) * 8 + p // 2


def selections():
    spread = np.zeros((48, 32), np.float32)
    shift = np.zeros((16, 16), np.float32)
    merge = np.zeros((32, 32), np.float32)
    for p in range(16):
        for e in range(3):
            if 2 * p - 1 + e >= 0:
                spread[e * 16 + rank_of(p), 2 * p - 1 + e] = 1
        if p < 15:
            shift[rank_of(p), rank_of(p + 1)] = 1
        for parity in range(2):
            merge[2 * p + parity, parity * 16 + rank_of(p)] = 1
    taps = np.zeros((3, 3, 8, 8, 16, 16), np.float32)
    moved = np.zeros((2, 2, 8, 8, 8, 8), np.float32)
    for p in range(8):
        for q in range(8):
            for e in range(3):
                for f in range(3):
                    j, l = 2 * p - 1 + e, 2 * q - 1 + f
                    if j >= 0 and l >= 0:
                        taps[e, f, q, p, l, rank_of(j)] = 1
            for a in range(2):
                for b in range(2):
                    if q + a < 8 and p + b < 8:
                        moved[a, b, q, p, q + a, p + b] = 1
    return tuple(
        m.astype(BF)
        for m in (
            np.kron(np.eye(8), spread),
            taps.reshape(576, 256),
            moved.reshape(256, 64),
            np.kron(np.eye(16), shift),
            np.kron(np.eye(8), merge),
        )
    )


def place():
    d, s = lax.axis_index("dp"), lax.axis_index("space")
    return d // 2, d % 2, s // (2 * NZ), (s // 2) % NZ, s % 2


def device(xl, core, y, z, xh):
    return {"dp": xl * 2 + core, "space": (y * NZ + z) * 2 + xh}


def remote(src, dst, sems, slot, target):
    copy = pltpu.make_async_remote_copy(
        src_ref=src,
        dst_ref=dst,
        send_sem=sems.at[0, slot],
        recv_sem=sems.at[1, slot],
        device_id=target,
        device_id_type=MESH,
    )
    copy.start()
    return copy


def dot(a, b, ca=1, cb=0):
    return lax.dot_general(a, b, (((ca,), (cb,)), ((), ())), preferred_element_type=F32)


def act_and_slope(v):
    t = jnp.exp(-jnp.abs(v))
    soft = jnp.maximum(v, 0.0) + jnp.log(1.0 + t)
    gate = jnp.where(v >= 0, 1.0, t) / (1.0 + t)
    return 0.2 * v + 0.8 * soft, 0.2 + 0.8 * gate


def far_first(n):
    return sorted(range(1, n), key=lambda k: -min(k, n - k))


class Reduction:
    def __init__(self, rows, s, bufs, sems, peers):
        self.rows, self.s, self.sems, self.peers = rows, s, sems, peers
        self.r1, self.hy, self.r2, self.hz, self.r3, self.kx, self.r4, self.g = bufs
        self.copies = []
        self.slot = 0
        self.at = place()

    def send(self, src, dst, target):
        copy = remote(src, dst, self.sems, self.slot, target)
        self.slot += 1
        self.copies.append(copy)
        return copy

    def cores(self):
        xl, core, y, z, xh = self.at
        self.order = sorted(range(1, NY), key=lambda k: min(k, NY - k)) + [0]
        self.first = {}
        for k in self.order:
            there = (y + k) % NY
            for h in range(2):
                self.first[k, h] = self.send(
                    self.s.at[h * 2 + 1 - core, pl.ds(there * NZ, NZ)], self.r1.at[k, h], self.peers["core"]
                )

    def along_y(self):
        xl, core, y, z, xh = self.at
        self.second = []
        for k in self.order:
            there = (y + k) % NY
            for h in range(2):
                self.first[k, h].wait_recv()

                @pl.loop(0, NZ)
                def _(i, h=h, k=k, there=there):
                    mine = self.s[h * 2 + core, there * NZ + i].astype(F32)
                    self.hy[k, h, i] = (mine + self.r1[k, h, i].astype(F32)).astype(BF)

            if k:
                self.second.append(self.send(self.hy.at[k], self.r2.at[k - 1], self.peers["y", k]))

    def along_z(self):
        xl, core, y, z, xh = self.at
        for copy in self.second:
            copy.wait_recv()
        self.third = []
        for k in far_first(NZ) + [0]:
            there = (z + k) % NZ
            for h in range(2):
                total = self.hy[0, h, there].astype(F32)
                for j in range(NY - 1):
                    total += self.r2[j, h, there].astype(F32)
                self.hz[k, h] = total.astype(BF)
            if k:
                self.third.append(self.send(self.hz.at[k], self.r3.at[k - 1], self.peers["z", k]))

    def along_x(self):
        xl, core, y, z, xh = self.at
        for copy in self.third:
            copy.wait_recv()
        for h in range(2):
            total = self.hz[0, h].astype(F32)
            for j in range(NZ - 1):
                total += self.r3[j, h].astype(F32)
            self.kx[h] = total.astype(BF)
        self.fourth = []
        for j, half in enumerate((1 - xl, xl, 1 - xl)):
            self.fourth.append(self.send(self.kx.at[half], self.r4.at[j], self.peers["x", j]))

    def gather_z(self):
        xl, core, y, z, xh = self.at
        total = self.kx[xl].astype(F32)
        for j, copy in enumerate(self.fourth):
            copy.wait_recv()
            total += self.r4[j].astype(F32)
        self.g[y, z] = total.astype(BF)
        self.fifth = []
        for k in far_first(NZ):
            self.fifth.append(self.send(self.g.at[y, z], self.g.at[y, z], self.peers["z", k]))

    def gather_y(self):
        xl, core, y, z, xh = self.at
        for copy in self.fifth:
            copy.wait_recv()
        self.sixth = []
        for k in far_first(NY):
            self.sixth.append(self.send(self.g.at[y], self.g.at[y], self.peers["y", k]))

    def finish(self):
        for copy in self.sixth:
            copy.wait_recv()

    def drain(self):
        for copy in self.copies:
            copy.wait_send()

    @staticmethod
    def scratch(rows):
        piece = rows // (NY * NZ)
        return [
            pltpu.VMEM((4, NY * NZ, piece, 128), BF),
            pltpu.VMEM((NY, 2, NZ, piece, 128), BF),
            pltpu.VMEM((NY, 2, NZ, piece, 128), BF),
            pltpu.VMEM((max(NY - 1, 1), 2, NZ, piece, 128), BF),
            pltpu.VMEM((NZ, 2, piece, 128), BF),
            pltpu.VMEM((NZ - 1, 2, piece, 128), BF),
            pltpu.VMEM((2, piece, 128), BF),
            pltpu.VMEM((3, piece, 128), BF),
            pltpu.VMEM((NY, NZ, piece, 128), BF),
            pltpu.SemaphoreType.DMA((2, 2 * NY + 2 * (NY - 1) + 2 * (NZ - 1) + 3)),
        ]


def step_kernel(scales, vol, w1, w2, cot, p0, p1, p2, p3, p4, actv, ig, g1out, g2out, *scratch):
    xe, xhalo, w1g, w1p, wb, w2g, hid, hhalo, slope, l2, d2, d2e, d1e, un = scratch[:14]
    wsem, hsem = scratch[14:16]
    s1, *bufs1, sems1 = scratch[16:26]
    s2, *bufs2, sems2 = scratch[26:36]
    at = xl, core, y, z, xh = place()
    s, d = lax.axis_index("space"), lax.axis_index("dp")
    n = 2 * NY * NZ
    bottom, top = s == 0, s == n - 1
    upper = {"space": (s + 1) % n}
    lower = {"space": (s + n - 1) % n}
    peers = {"core": device(xl, 1 - core, y, z, xh)}
    for k in range(1, NY):
        peers["y", k] = device(xl, core, (y + k) % NY, z, xh)
    for k in range(1, NZ):
        peers["z", k] = device(xl, core, y, (z + k) % NZ, xh)
    peers["x", 0] = device(1 - xl, core, y, z, xh)
    peers["x", 1] = device(xl, core, y, z, 1 - xh)
    peers["x", 2] = device(1 - xl, core, y, z, 1 - xh)
    peers["upper"], peers["lower"] = upper, lower

    barrier = pltpu.get_barrier_semaphore()
    for peer in peers.values():
        pl.semaphore_signal(barrier, inc=1, device_id=peer, device_id_type=MESH)
    pl.semaphore_wait(barrier, len(peers))

    def rows(q, size, lo, hi):
        return pl.ds(pl.multiple_of(q * size + lo, 16), hi - lo)

    sent = []
    forward = []
    theirs = (1 - xl) * 2 + core
    for slot, (own, whole, size, cut) in enumerate(((w1, w1g, 432, 224), (w2, w2g, 864, 432))):
        base = slot * 5
        parts = ((0, cut, peers["x", 0]), (cut, size, peers["x", 2]))
        arriving = []
        for j, (lo, hi, peer) in enumerate(parts):
            arriving.append(remote(own.at[pl.ds(lo, hi - lo)], whole.at[rows(d, size, lo, hi)], wsem, base + j, peer))
        to_core = remote(own, whole.at[rows(d, size, 0, size)], wsem, base + 2, peers["core"])
        forward.append((whole, size, parts, arriving, to_core, base))
        sent += arriving + [to_core]
        if slot == 0:
            halo_in = remote(vol.at[pl.ds(224, 32)], xhalo, hsem, 0, upper)

    passed = []

    def pass_on(slot):
        whole, size, parts, arriving, to_core, base = forward[slot]
        for j, (lo, hi, _) in enumerate(parts):
            arriving[j].wait_recv()
            part = whole.at[rows(theirs, size, lo, hi)]
            passed.append(remote(part, part, wsem, base + 3 + j, peers["core"]))
        return to_core, passed[-2:]

    xe[:, :, 0] = jnp.zeros((9, 3, 16, 128), BF)

    @pl.loop(0, 8)
    def _(c):
        got = dot(p0[...], vol[:, pl.ds(pl.multiple_of(c * 256, 256), 256)]).astype(BF)
        for i in range(8):
            for e in range(3):
                for u in range(2):
                    xe[i + 1, e, 2 * c + 1 + u] = got[(i * 3 + e) * 16 : (i * 3 + e + 1) * 16, u * 128 : (u + 1) * 128]

    w1g[rows(d, 432, 0, 432)] = w1[...]
    w2g[rows(d, 864, 0, 864)] = w2[...]
    to_core, others = pass_on(0)
    to_core.wait_recv()
    for copy in others:
        copy.wait_recv()
    for t in range(9):
        w1p[t * 256 : t * 256 + 64] = jnp.zeros((64, 128), BF)
        w1p[t * 256 + 64 : t * 256 + 256] = w1g[t * 192 : (t + 1) * 192]

    def conv_first(o):
        tiles = []
        for a in range(3):
            for e in range(3):
                tiles.append(xe[2 * o + a, e, 0:16].reshape(256, 128))
                tiles.append(xe[2 * o + a, e, 1:17].reshape(256, 128))
        value, gate = act_and_slope(dot(jnp.concatenate(tiles, axis=1), w1p[...]))
        hid[o] = value.astype(BF)
        slope[o] = gate.reshape(16, 16, 128)

    conv_first(3)
    halo_hid = remote(hid.at[3], hhalo, hsem, 1, upper)
    to_core_second, others_second = pass_on(1)

    @pl.loop(1, 3)
    def _(o):
        conv_first(o)

    halo_in.wait_recv()
    rim = jnp.where(bottom, jnp.zeros_like(xhalo), xhalo[...])
    got = dot(p0[0:48, 0:32], rim).astype(BF)
    for e in range(3):
        for u in range(16):
            xe[0, e, u + 1] = got[e * 16 : (e + 1) * 16, u * 128 : (u + 1) * 128]
    conv_first(0)

    def place_taps(got, plane):
        for o in range(2):
            a = plane - 2 * o
            if 0 <= a < 3:
                for k in range(9):
                    l2[o * 64 : (o + 1) * 64, (a * 9 + k) * 128 : (a * 9 + k + 1) * 128] = got[k * 64 : (k + 1) * 64]

    for pair in range(2):
        both = jnp.concatenate([hid[2 * pair], hid[2 * pair + 1]], axis=1)
        got = dot(p1[...], both).astype(BF)
        place_taps(got[:, :128], 2 * pair + 1)
        place_taps(got[:, 128:], 2 * pair + 2)
    for t in range(9):
        block = w1p[t * 256 : (t + 1) * 256]
        wb[t * 256 : t * 256 + 128] = block[128:].T
        wb[t * 256 + 128 : (t + 1) * 256] = block[:128].T
    halo_hid.wait_recv()
    rim = jnp.where(bottom, jnp.zeros_like(hhalo), hhalo[...])
    place_taps(dot(p1[...], rim).astype(BF), 0)
    to_core_second.wait_recv()
    for copy in others_second:
        copy.wait_recv()

    linear = dot(l2[...], w2g[...])
    value, gate = act_and_slope(linear)
    arriving = jnp.concatenate(
        [cot[o, :, q * 256 : (q + 1) * 256].astype(F32) for o in range(2) for q in range(8)], axis=0
    )
    delta = (arriving * gate).astype(BF)
    d2[0] = delta[:64]
    halo_d2 = remote(d2.at[0], d2.at[2], hsem, 2, lower)
    d2[1] = delta[64:]
    for o in range(2):
        for q in range(8):
            at_row = (o * 8 + q) * 8
            actv[o, :, q * 256 : (q + 1) * 256] = value[at_row : at_row + 8].astype(BF)

    piece1, piece2 = R1ROWS // (NY * NZ), R2ROWS // (NY * NZ)
    s2[:, 1728 // piece2 :] = jnp.zeros((4, NY * NZ - 1728 // piece2, piece2, 128), BF)
    s1[:, 432 // piece1 :] = jnp.zeros((4, NY * NZ - 432 // piece1, piece1, 128), BF)
    for t in range(27):
        got = dot(l2[:, t * 128 : (t + 1) * 128], delta, 0, 0).astype(BF)
        for k in range(4):
            row = t * 128 + 32 * k
            for half in range(2):
                flat = half * 864 + row % 864
                s2[row // 864, flat // piece2, flat % piece2 : flat % piece2 + 32] = got[
                    32 * k : 32 * k + 32, half * 128 : (half + 1) * 128
                ]
    sum2 = Reduction(R2ROWS, s2, bufs2, sems2, peers)
    sum1 = Reduction(R1ROWS, s1, bufs1, sems1, peers)
    sum2.cores()

    def spread_delta(o):
        got = dot(p2[...], d2[o]).astype(BF)
        for v in range(4):
            d2e[o, v] = got[v * 64 : (v + 1) * 64]

    taps_of = (((1, 0),), ((2, 0), (0, 1)))

    def hidden_delta(pi):
        for pq in range(2):
            halves = []
            for pj in range(2):
                left, right = [], []
                for a, sa in taps_of[pi]:
                    for e, se in taps_of[pj]:
                        for f, sf in taps_of[pq]:
                            left.append(d2e[sa : sa + 2, sf * 2 + se].reshape(128, 256))
                            t = a * 9 + e * 3 + f
                            right.append(w2g[t * 128 : (t + 1) * 128])
                got = dot(jnp.concatenate(left, axis=1), jnp.concatenate(right, axis=1), 1, 1)
                halves.append(got.reshape(2, 8, 8, 128))
            both = jnp.concatenate(halves, axis=2)
            for i in range(2):
                for q in range(8):
                    d1e[2 * i + pi, 0, 2 * q + pq] = (both[i, q] * slope[2 * i + pi, 2 * q + pq]).astype(BF)

    spread_delta(0)
    spread_delta(1)
    d1e[:, :, 16] = jnp.zeros((5, 2, 16, 128), BF)
    hidden_delta(0)
    halo_d1 = remote(d1e.at[0, 0, pl.ds(0, 16)], d1e.at[4, 0, pl.ds(0, 16)], hsem, 3, lower)
    sum2.along_y()
    halo_d2.wait_recv()
    d2[2] = jnp.where(top, jnp.zeros((64, 256), BF), d2[2])
    spread_delta(2)
    hidden_delta(1)

    flat1 = jnp.concatenate([d1e[o, 0, 0:16].reshape(256, 128) for o in range(4)], axis=0)

    @pl.loop(0, 9)
    def _(t):
        a, e = t // 3, t % 3
        left = jnp.concatenate(
            [
                jnp.concatenate(
                    [xe[2 * o + a, e, 0:16].reshape(256, 128), xe[2 * o + a, e, 1:17].reshape(256, 128)], axis=1
                )
                for o in range(4)
            ],
            axis=0,
        )
        got = dot(left, flat1, 0, 0).astype(BF)
        for k in range(12):
            block = t * 12 + k
            row = (block % 27) * 16
            s1[block // 27, row // piece1, pl.ds(pl.multiple_of(row % piece1, 16), 16)] = got[
                64 + k * 16 : 64 + (k + 1) * 16
            ]

    sum1.cores()
    sum2.along_z()

    def shift_delta(first, count):
        both = jnp.concatenate([d1e[first + k, 0, 0:16].reshape(256, 128) for k in range(count)], axis=1)
        got = dot(p3[...], both).astype(BF)
        for k in range(count):
            d1e[first + k, 1, 0:16] = got[:, k * 128 : (k + 1) * 128].reshape(16, 16, 128)

    def input_delta(pi, pj):
        @pl.loop(0, 4)
        def _(i):
            left, right = [], []
            for a, sa in taps_of[pi]:
                for e, se in taps_of[pj]:
                    left.append(d1e[i + sa, se, 0:16].reshape(256, 128))
                    left.append(d1e[i + sa, se, 1:17].reshape(256, 128))
                    t = a * 3 + e
                    right.append(wb[t * 256 : (t + 1) * 256])
            got = dot(jnp.concatenate(left, axis=1), jnp.concatenate(right, axis=0)).astype(BF)
            for q in range(16):
                un[2 * i + pi, pj * 16 : (pj + 1) * 16, q * 128 : (q + 1) * 128] = got[q * 16 : (q + 1) * 16]

    shift_delta(0, 2)
    shift_delta(2, 2)
    sum1.along_y()
    input_delta(0, 0)
    sum2.along_x()
    input_delta(0, 1)
    sum1.along_z()
    sum2.gather_z()
    halo_d1.wait_recv()
    d1e[4, 0, 0:16] = jnp.where(top, jnp.zeros((16, 16, 128), BF), d1e[4, 0, 0:16])
    shift_delta(4, 1)
    input_delta(1, 0)
    sum1.along_x()
    sum2.gather_y()
    input_delta(1, 1)
    sum1.gather_z()

    @pl.loop(0, 8)
    def _(c):
        lanes = pl.ds(pl.multiple_of(c * 256, 256), 256)
        ig[:, lanes] = dot(p4[...], un[:, :, lanes].reshape(256, 256)).astype(BF)

    sum1.gather_y()
    sum2.finish()
    whole = bufs2[-1]
    for block in range(54):
        flat = block * 32
        k = flat // piece2
        got = whole[k // NZ, k % NZ, flat % piece2 : flat % piece2 + 32].astype(F32) * scales[1]
        g2out[flat % 864 : flat % 864 + 32, flat // 864 * 128 : (flat // 864 + 1) * 128] = got
    sum1.finish()
    whole = bufs1[-1]
    for block in range(27):
        flat = block * 16
        k = flat // piece1
        g1out[flat : flat + 16] = whole[k // NZ, k % NZ, flat % piece1 : flat % piece1 + 16].astype(F32) * scales[0]

    for copy in sent + passed + [halo_in, halo_hid, halo_d2, halo_d1]:
        copy.wait_send()
    sum2.drain()
    sum1.drain()


def local(volume, weight_first, weight_second, cotangent):
    cells = 4 * lax.axis_size("space") * 4 * 256
    scales = (float(cells) ** -0.5, float(cells // 8) ** -0.5)
    vmem = pl.BlockSpec(memory_space=pltpu.VMEM)
    shape = jax.ShapeDtypeStruct

    def body(*refs):
        step_kernel(scales, *refs)

    activations, input_gradient, first, second = pl.pallas_call(
        body,
        out_shape=(
            shape((2, 8, 2048), BF),
            shape((256, 2048), BF),
            shape((432, 128), F32),
            shape((864, 256), F32),
        ),
        in_specs=[vmem] * 9,
        out_specs=(vmem,) * 4,
        scratch_shapes=[
            pltpu.VMEM((9, 3, 17, 16, 128), BF),
            pltpu.VMEM((32, 2048), BF),
            pltpu.VMEM((1728, 128), BF),
            pltpu.VMEM((2304, 128), BF),
            pltpu.VMEM((2304, 128), BF),
            pltpu.VMEM((3456, 256), BF),
            pltpu.VMEM((4, 256, 128), BF),
            pltpu.VMEM((256, 128), BF),
            pltpu.VMEM((4, 16, 16, 128), F32),
            pltpu.VMEM((128, 3456), BF),
            pltpu.VMEM((3, 64, 256), BF),
            pltpu.VMEM((3, 4, 64, 256), BF),
            pltpu.VMEM((5, 2, 17, 16, 128), BF),
            pltpu.VMEM((8, 32, 2048), BF),
            pltpu.SemaphoreType.DMA((2, 10)),
            pltpu.SemaphoreType.DMA((2, 4)),
        ]
        + Reduction.scratch(R1ROWS)
        + Reduction.scratch(R2ROWS),
        compiler_params=pltpu.CompilerParams(
            collective_id=0, has_side_effects=True, vmem_limit_bytes=60 * 1024 * 1024
        ),
        name="step",
    )(
        volume.reshape(256, 2048),
        weight_first,
        weight_second,
        cotangent.reshape(2, 8, 2048),
        *selections(),
    )
    return (
        activations.reshape(cotangent.shape),
        input_gradient.reshape(volume.shape),
        first,
        second,
    )


def solution(mesh):
    return jax.shard_map(
        local,
        mesh=mesh,
        in_specs=(
            P("dp", "space", None, None),
            P("dp", None),
            P("dp", None),
            P("dp", "space", None, None),
        ),
        out_specs=(
            P("dp", "space", None, None),
            P("dp", "space", None, None),
            P("dp", None),
            P("dp", None),
        ),
        check_vma=False,
    )
```

```python
import numpy as np

import jax
import jax.numpy as jnp
from jax import lax
from jax.experimental import pallas as pl
from jax.experimental.pallas import tpu as pltpu
from jax.sharding import PartitionSpec as P

NY, NZ = 4, 8
BF, F32 = jnp.bfloat16, jnp.float32
PIECE1, PIECE2 = 8, 32
GROUP1, GROUP2 = 56, 216
USED = 7
MESH = pl.DeviceIdType.MESH


def rank_of(p):
    return (p % 2) * 8 + p // 2


def selections():
    spread = np.zeros((48, 32), np.float32)
    shift = np.zeros((16, 16), np.float32)
    merge = np.zeros((32, 32), np.float32)
    for p in range(16):
        for e in range(3):
            if 2 * p - 1 + e >= 0:
                spread[e * 16 + rank_of(p), 2 * p - 1 + e] = 1
        if p < 15:
            shift[rank_of(p), rank_of(p + 1)] = 1
        for parity in range(2):
            merge[2 * p + parity, parity * 16 + rank_of(p)] = 1
    taps = np.zeros((3, 3, 8, 8, 16, 16), np.float32)
    moved = np.zeros((2, 2, 8, 8, 8, 8), np.float32)
    for p in range(8):
        for q in range(8):
            for e in range(3):
                for f in range(3):
                    j, l = 2 * p - 1 + e, 2 * q - 1 + f
                    if j >= 0 and l >= 0:
                        taps[e, f, q, p, l, rank_of(j)] = 1
            for a in range(2):
                for b in range(2):
                    if q + a < 8 and p + b < 8:
                        moved[a, b, q, p, q + a, p + b] = 1
    return tuple(
        m.astype(BF)
        for m in (
            np.kron(np.eye(8), spread),
            taps.reshape(576, 256),
            moved.reshape(256, 64),
            np.kron(np.eye(16), shift),
            np.kron(np.eye(8), merge),
        )
    )


def place():
    d, s = lax.axis_index("dp"), lax.axis_index("space")
    return d // 2, d % 2, s // (2 * NZ), (s // 2) % NZ, s % 2


def device(xl, core, y, z, xh):
    return {"dp": xl * 2 + core, "space": (y * NZ + z) * 2 + xh}


def remote(src, dst, sems, slot, target):
    copy = pltpu.make_async_remote_copy(
        src_ref=src,
        dst_ref=dst,
        send_sem=sems.at[0, slot],
        recv_sem=sems.at[1, slot],
        device_id=target,
        device_id_type=MESH,
    )
    copy.start()
    return copy


def dot(a, b, ca=1, cb=0):
    return lax.dot_general(a, b, (((ca,), (cb,)), ((), ())), preferred_element_type=F32)


def act_and_slope(v):
    t = jnp.exp(-jnp.abs(v))
    soft = jnp.maximum(v, 0.0) + jnp.log(1.0 + t)
    gate = jnp.where(v >= 0, 1.0, t) / (1.0 + t)
    return 0.2 * v + 0.8 * soft, 0.2 + 0.8 * gate


def far_first(n):
    return sorted(range(1, n), key=lambda k: -min(k, n - k))


class Reduction:
    def __init__(self, s, bufs, sems, peers):
        self.s, self.sems, self.peers = s, sems, peers
        self.r1, self.hy, self.r2, self.hz, self.r3, self.g = bufs
        self.copies = []
        self.slot = 0
        self.at = place()

    def send(self, src, dst, target):
        copy = remote(src, dst, self.sems, self.slot, target)
        self.slot += 1
        self.copies.append(copy)
        return copy

    def cores(self):
        xl, core, y, z, xh = self.at
        self.order = far_first(NY) + [0]
        self.first = {}
        for k in self.order:
            there = (y + k) % NY
            for h in range(2):
                self.first[k, h] = self.send(
                    self.s.at[h * 2 + 1 - core, there, :, pl.ds(0, USED)],
                    self.r1.at[k, h, :, pl.ds(0, USED)],
                    self.peers["core"],
                )

    def plane(self):
        xl, core, y, z, xh = self.at
        self.second = []
        for k in self.order:
            there = (y + k) % NY
            for h in range(2):
                self.first[k, h].wait_recv()
            for h in range(2):
                for v in range(2):
                    left = xl + h - 2 * xl * h
                    half = xh + v - 2 * xh * v
                    for i in range(USED):
                        mine = self.s[left * 2 + core, there, half, i].astype(F32)
                        self.hy[k, h, v, i] = (mine + self.r1[k, left, half, i].astype(F32)).astype(BF)
                    if (k, h, v) != (0, 0, 0):
                        self.second.append(
                            self.send(
                                self.hy.at[k, h, v, pl.ds(0, USED)],
                                self.r2.at[k, h, v, pl.ds(0, USED)],
                                self.peers["plane", k, h, v],
                            )
                        )

    def along_z(self):
        xl, core, y, z, xh = self.at
        for copy in self.second:
            copy.wait_recv()
        self.third = []
        for k in far_first(NZ) + [0]:
            there = (z + k) % NZ
            total = self.hy[0, 0, 0, there].astype(F32)
            for j in range(NY):
                for h in range(2):
                    for v in range(2):
                        if (j, h, v) != (0, 0, 0):
                            total += self.r2[j, h, v, there].astype(F32)
            self.hz[k] = total.astype(BF)
            if k:
                self.third.append(self.send(self.hz.at[k], self.r3.at[k - 1], self.peers["z", k]))

    def gather_z(self):
        xl, core, y, z, xh = self.at
        for copy in self.third:
            copy.wait_recv()
        total = self.hz[0].astype(F32)
        for j in range(NZ - 1):
            total += self.r3[j].astype(F32)
        self.g[y, xh, z] = total.astype(BF)
        self.fifth = []
        for k in far_first(NZ):
            self.fifth.append(self.send(self.g.at[y, xh, z], self.g.at[y, xh, z], self.peers["z", k]))

    def gather_plane(self):
        xl, core, y, z, xh = self.at
        for copy in self.fifth:
            copy.wait_recv()
        self.sixth = []
        part = self.g.at[y, xh, pl.ds(0, USED)]
        for k in far_first(NY) + [0]:
            for v in (1, 0):
                if (k, v) != (0, 0):
                    self.sixth.append(self.send(part, part, self.peers["plane", k, 0, v]))

    def finish(self):
        for copy in self.sixth:
            copy.wait_recv()

    def drain(self):
        for copy in self.copies:
            copy.wait_send()

    @staticmethod
    def scratch(piece):
        blocks = (NY, 2, 2, NZ, piece, 128)
        return [
            pltpu.VMEM((4, NY, 2, NZ, piece, 128), BF),
            pltpu.VMEM(blocks, BF),
            pltpu.VMEM(blocks, BF),
            pltpu.VMEM(blocks, BF),
            pltpu.VMEM((NZ, piece, 128), BF),
            pltpu.VMEM((NZ - 1, piece, 128), BF),
            pltpu.VMEM((NY, 2, NZ, piece, 128), BF),
            pltpu.SemaphoreType.DMA((2, 2 * NY + (4 * NY - 1) + 2 * (NZ - 1) + (2 * NY - 1))),
        ]


def step_kernel(scales, vol, w1, w2, cot, p0, p1, p2, p3, p4, actv, ig, g1out, g2out, *scratch):
    xe, xhalo, w1g, w1p, wb, w2g, hid, hhalo, slope, l2, d2, d2e, d1e, un = scratch[:14]
    wsem, hsem = scratch[14:16]
    s1, *bufs1, sems1 = scratch[16:24]
    s2, *bufs2, sems2 = scratch[24:32]
    at = xl, core, y, z, xh = place()
    s, d = lax.axis_index("space"), lax.axis_index("dp")
    n = 2 * NY * NZ
    bottom, top = s == 0, s == n - 1
    upper = {"space": (s + 1) % n}
    lower = {"space": (s + n - 1) % n}
    peers = {"core": device(xl, 1 - core, y, z, xh)}
    for k in range(NY):
        for h in range(2):
            for v in range(2):
                if (k, h, v) != (0, 0, 0):
                    there = xl + h - 2 * xl * h, core, (y + k) % NY, z, xh + v - 2 * xh * v
                    peers["plane", k, h, v] = device(*there)
    for k in range(1, NZ):
        peers["z", k] = device(xl, core, y, (z + k) % NZ, xh)
    peers["upper"], peers["lower"] = upper, lower

    barrier = pltpu.get_barrier_semaphore()
    for peer in peers.values():
        pl.semaphore_signal(barrier, inc=1, device_id=peer, device_id_type=MESH)
    pl.semaphore_wait(barrier, len(peers))

    def rows(q, size, lo, hi):
        return pl.ds(pl.multiple_of(q * size + lo, 16), hi - lo)

    sent = []
    forward = []
    theirs = (1 - xl) * 2 + core
    for slot, (own, whole, size, cut) in enumerate(((w1, w1g, 432, 224), (w2, w2g, 864, 432))):
        base = slot * 5
        parts = ((0, cut, peers["plane", 0, 1, 0]), (cut, size, peers["plane", 0, 1, 1]))
        arriving = []
        for j, (lo, hi, peer) in enumerate(parts):
            arriving.append(remote(own.at[pl.ds(lo, hi - lo)], whole.at[rows(d, size, lo, hi)], wsem, base + j, peer))
        to_core = remote(own, whole.at[rows(d, size, 0, size)], wsem, base + 2, peers["core"])
        forward.append((whole, size, parts, arriving, to_core, base))
        sent += arriving + [to_core]
        if slot == 0:
            halo_in = remote(vol.at[pl.ds(224, 32)], xhalo, hsem, 0, upper)

    passed = []

    def pass_on(slot):
        whole, size, parts, arriving, to_core, base = forward[slot]
        for j, (lo, hi, _) in enumerate(parts):
            arriving[j].wait_recv()
            part = whole.at[rows(theirs, size, lo, hi)]
            passed.append(remote(part, part, wsem, base + 3 + j, peers["core"]))
        return to_core, passed[-2:]

    xe[:, :, 0] = jnp.zeros((9, 3, 16, 128), BF)

    @pl.loop(0, 8)
    def _(c):
        got = dot(p0[...], vol[:, pl.ds(pl.multiple_of(c * 256, 256), 256)]).astype(BF)
        for i in range(8):
            for e in range(3):
                for u in range(2):
                    xe[i + 1, e, 2 * c + 1 + u] = got[(i * 3 + e) * 16 : (i * 3 + e + 1) * 16, u * 128 : (u + 1) * 128]

    w1g[rows(d, 432, 0, 432)] = w1[...]
    w2g[rows(d, 864, 0, 864)] = w2[...]
    to_core, others = pass_on(0)
    to_core.wait_recv()
    for copy in others:
        copy.wait_recv()
    for t in range(9):
        w1p[t * 256 : t * 256 + 64] = jnp.zeros((64, 128), BF)
        w1p[t * 256 + 64 : t * 256 + 256] = w1g[t * 192 : (t + 1) * 192]

    def conv_first(o):
        tiles = []
        for a in range(3):
            for e in range(3):
                tiles.append(xe[2 * o + a, e, 0:16].reshape(256, 128))
                tiles.append(xe[2 * o + a, e, 1:17].reshape(256, 128))
        value, gate = act_and_slope(dot(jnp.concatenate(tiles, axis=1), w1p[...]))
        hid[o] = value.astype(BF)
        slope[o] = gate.reshape(16, 16, 128)

    conv_first(3)
    halo_hid = remote(hid.at[3], hhalo, hsem, 1, upper)
    to_core_second, others_second = pass_on(1)

    @pl.loop(1, 3)
    def _(o):
        conv_first(o)

    halo_in.wait_recv()
    rim = jnp.where(bottom, jnp.zeros_like(xhalo), xhalo[...])
    got = dot(p0[0:48, 0:32], rim).astype(BF)
    for e in range(3):
        for u in range(16):
            xe[0, e, u + 1] = got[e * 16 : (e + 1) * 16, u * 128 : (u + 1) * 128]
    conv_first(0)

    def place_taps(got, plane):
        for o in range(2):
            a = plane - 2 * o
            if 0 <= a < 3:
                for k in range(9):
                    l2[o * 64 : (o + 1) * 64, (a * 9 + k) * 128 : (a * 9 + k + 1) * 128] = got[k * 64 : (k + 1) * 64]

    for pair in range(2):
        both = jnp.concatenate([hid[2 * pair], hid[2 * pair + 1]], axis=1)
        got = dot(p1[...], both).astype(BF)
        place_taps(got[:, :128], 2 * pair + 1)
        place_taps(got[:, 128:], 2 * pair + 2)
    for t in range(9):
        block = w1p[t * 256 : (t + 1) * 256]
        wb[t * 256 : t * 256 + 128] = block[128:].T
        wb[t * 256 + 128 : (t + 1) * 256] = block[:128].T
    halo_hid.wait_recv()
    rim = jnp.where(bottom, jnp.zeros_like(hhalo), hhalo[...])
    place_taps(dot(p1[...], rim).astype(BF), 0)
    to_core_second.wait_recv()
    for copy in others_second:
        copy.wait_recv()

    linear = dot(l2[...], w2g[...])
    value, gate = act_and_slope(linear)
    arriving = jnp.concatenate(
        [cot[o, :, q * 256 : (q + 1) * 256].astype(F32) for o in range(2) for q in range(8)], axis=0
    )
    delta = (arriving * gate).astype(BF)
    d2[0] = delta[:64]
    halo_d2 = remote(d2.at[0], d2.at[2], hsem, 2, lower)
    d2[1] = delta[64:]
    for o in range(2):
        for q in range(8):
            at_row = (o * 8 + q) * 8
            actv[o, :, q * 256 : (q + 1) * 256] = value[at_row : at_row + 8].astype(BF)

    def pieces(lo, hi, group, piece):
        while lo < hi:
            where = lo % group
            count = min(hi - lo, group - where, piece - where % piece)
            yield lo, count, lo // group, where // piece, where % piece
            lo += count

    for t in range(27):
        got = dot(l2[:, t * 128 : (t + 1) * 128], delta, 0, 0)
        for q in range(4):
            lo, hi = max(t * 128, q * 864), min(t * 128 + 128, q * 864 + 864)
            for row, count, g, k, at_row in pieces(lo - q * 864, hi - q * 864, GROUP2, PIECE2):
                row += q * 864 - t * 128
                for half in range(2):
                    block = got[row : row + count, half * 128 : (half + 1) * 128].astype(BF)
                    h = half * NY + g
                    s2[q, h // 2, h % 2, k, at_row : at_row + count] = block
    sum2 = Reduction(s2, bufs2, sems2, peers)
    sum1 = Reduction(s1, bufs1, sems1, peers)
    sum2.cores()

    def spread_delta(o):
        got = dot(p2[...], d2[o]).astype(BF)
        for v in range(4):
            d2e[o, v] = got[v * 64 : (v + 1) * 64]

    taps_of = (((1, 0),), ((2, 0), (0, 1)))

    def hidden_delta(pi):
        for pq in range(2):
            halves = []
            for pj in range(2):
                left, right = [], []
                for a, sa in taps_of[pi]:
                    for e, se in taps_of[pj]:
                        for f, sf in taps_of[pq]:
                            left.append(d2e[sa : sa + 2, sf * 2 + se].reshape(128, 256))
                            t = a * 9 + e * 3 + f
                            right.append(w2g[t * 128 : (t + 1) * 128])
                got = dot(jnp.concatenate(left, axis=1), jnp.concatenate(right, axis=1), 1, 1)
                halves.append(got.reshape(2, 8, 8, 128))
            both = jnp.concatenate(halves, axis=2)
            for i in range(2):
                for q in range(8):
                    d1e[2 * i + pi, 0, 2 * q + pq] = (both[i, q] * slope[2 * i + pi, 2 * q + pq]).astype(BF)

    spread_delta(0)
    spread_delta(1)
    d1e[:, :, 16] = jnp.zeros((5, 2, 16, 128), BF)
    hidden_delta(0)
    halo_d1 = remote(d1e.at[0, 0, pl.ds(0, 16)], d1e.at[4, 0, pl.ds(0, 16)], hsem, 3, lower)
    sum2.plane()
    halo_d2.wait_recv()
    d2[2] = jnp.where(top, jnp.zeros((64, 256), BF), d2[2])
    spread_delta(2)
    hidden_delta(1)

    flat1 = jnp.concatenate([d1e[o, 0, 0:16].reshape(256, 128) for o in range(4)], axis=0)

    @pl.loop(0, 9)
    def _(t):
        a, e = t // 3, t % 3
        left = jnp.concatenate(
            [
                jnp.concatenate(
                    [xe[2 * o + a, e, 0:16].reshape(256, 128), xe[2 * o + a, e, 1:17].reshape(256, 128)], axis=1
                )
                for o in range(4)
            ],
            axis=0,
        )
        got = dot(left, flat1, 0, 0)
        for k in range(24):
            block = t * 24 + k
            g = block % 54 // 7
            s1[block // 54, g // 2, g % 2, block % 54 % 7] = got[64 + k * 8 : 64 + (k + 1) * 8].astype(BF)

    sum1.cores()
    sum2.along_z()

    def shift_delta(first, count):
        both = jnp.concatenate([d1e[first + k, 0, 0:16].reshape(256, 128) for k in range(count)], axis=1)
        got = dot(p3[...], both).astype(BF)
        for k in range(count):
            d1e[first + k, 1, 0:16] = got[:, k * 128 : (k + 1) * 128].reshape(16, 16, 128)

    def input_delta(pi, pj):
        @pl.loop(0, 4)
        def _(i):
            left, right = [], []
            for a, sa in taps_of[pi]:
                for e, se in taps_of[pj]:
                    left.append(d1e[i + sa, se, 0:16].reshape(256, 128))
                    left.append(d1e[i + sa, se, 1:17].reshape(256, 128))
                    t = a * 3 + e
                    right.append(wb[t * 256 : (t + 1) * 256])
            got = dot(jnp.concatenate(left, axis=1), jnp.concatenate(right, axis=0)).astype(BF)
            for q in range(16):
                un[2 * i + pi, pj * 16 : (pj + 1) * 16, q * 128 : (q + 1) * 128] = got[q * 16 : (q + 1) * 16]

    shift_delta(0, 2)
    shift_delta(2, 2)
    sum1.plane()
    input_delta(0, 0)
    input_delta(0, 1)
    sum1.along_z()
    sum2.gather_z()
    halo_d1.wait_recv()
    d1e[4, 0, 0:16] = jnp.where(top, jnp.zeros((16, 16, 128), BF), d1e[4, 0, 0:16])
    shift_delta(4, 1)
    input_delta(1, 0)
    sum2.gather_plane()
    input_delta(1, 1)
    sum1.gather_z()

    @pl.loop(0, 8)
    def _(c):
        lanes = pl.ds(pl.multiple_of(c * 256, 256), 256)
        ig[:, lanes] = dot(p4[...], un[:, :, lanes].reshape(256, 256)).astype(BF)

    sum1.gather_plane()
    sum2.finish()
    whole = bufs2[-1]
    for row, count, g, k, at_row in pieces(0, 1728, GROUP2, PIECE2):
        got = whole[g // 2, g % 2, k, at_row : at_row + count].astype(F32) * scales[1]
        half = row // 864
        g2out[row % 864 : row % 864 + count, half * 128 : (half + 1) * 128] = got
    sum1.finish()
    whole = bufs1[-1]
    for row, count, g, k, at_row in pieces(0, 432, GROUP1, PIECE1):
        g1out[row : row + count] = whole[g // 2, g % 2, k].astype(F32) * scales[0]

    for copy in sent + passed + [halo_in, halo_hid, halo_d2, halo_d1]:
        copy.wait_send()
    sum2.drain()
    sum1.drain()


def local(volume, weight_first, weight_second, cotangent):
    cells = 4 * lax.axis_size("space") * 4 * 256
    scales = (float(cells) ** -0.5, float(cells // 8) ** -0.5)
    vmem = pl.BlockSpec(memory_space=pltpu.VMEM)
    shape = jax.ShapeDtypeStruct

    def body(*refs):
        step_kernel(scales, *refs)

    activations, input_gradient, first, second = pl.pallas_call(
        body,
        out_shape=(
            shape((2, 8, 2048), BF),
            shape((256, 2048), BF),
            shape((432, 128), F32),
            shape((864, 256), F32),
        ),
        in_specs=[vmem] * 9,
        out_specs=(vmem,) * 4,
        scratch_shapes=[
            pltpu.VMEM((9, 3, 17, 16, 128), BF),
            pltpu.VMEM((32, 2048), BF),
            pltpu.VMEM((1728, 128), BF),
            pltpu.VMEM((2304, 128), BF),
            pltpu.VMEM((2304, 128), BF),
            pltpu.VMEM((3456, 256), BF),
            pltpu.VMEM((4, 256, 128), BF),
            pltpu.VMEM((256, 128), BF),
            pltpu.VMEM((4, 16, 16, 128), F32),
            pltpu.VMEM((128, 3456), BF),
            pltpu.VMEM((3, 64, 256), BF),
            pltpu.VMEM((3, 4, 64, 256), BF),
            pltpu.VMEM((5, 2, 17, 16, 128), BF),
            pltpu.VMEM((8, 32, 2048), BF),
            pltpu.SemaphoreType.DMA((2, 10)),
            pltpu.SemaphoreType.DMA((2, 4)),
        ]
        + Reduction.scratch(PIECE1)
        + Reduction.scratch(PIECE2),
        compiler_params=pltpu.CompilerParams(
            collective_id=0, has_side_effects=True, vmem_limit_bytes=60 * 1024 * 1024
        ),
        name="step",
    )(
        volume.reshape(256, 2048),
        weight_first,
        weight_second,
        cotangent.reshape(2, 8, 2048),
        *selections(),
    )
    return (
        activations.reshape(cotangent.shape),
        input_gradient.reshape(volume.shape),
        first,
        second,
    )


def solution(mesh):
    return jax.shard_map(
        local,
        mesh=mesh,
        in_specs=(
            P("dp", "space", None, None),
            P("dp", None),
            P("dp", None),
            P("dp", "space", None, None),
        ),
        out_specs=(
            P("dp", "space", None, None),
            P("dp", "space", None, None),
            P("dp", None),
            P("dp", None),
        ),
        check_vma=False,
    )
```

```python
import numpy as np

import jax
import jax.numpy as jnp
from jax import lax
from jax.experimental import pallas as pl
from jax.experimental.pallas import tpu as pltpu
from jax.sharding import PartitionSpec as P

NY, NZ = 4, 8
BF, F32 = jnp.bfloat16, jnp.float32
PIECE1, PIECE2 = 8, 32
GROUP1, GROUP2 = 56, 216
USED = 7
MESH = pl.DeviceIdType.MESH


def rank_of(p):
    return (p % 2) * 8 + p // 2


def selections():
    spread = np.zeros((48, 32), np.float32)
    shift = np.zeros((16, 16), np.float32)
    merge = np.zeros((32, 32), np.float32)
    for p in range(16):
        for e in range(3):
            if 2 * p - 1 + e >= 0:
                spread[e * 16 + rank_of(p), 2 * p - 1 + e] = 1
        if p < 15:
            shift[rank_of(p), rank_of(p + 1)] = 1
        for parity in range(2):
            merge[2 * p + parity, parity * 16 + rank_of(p)] = 1
    taps = np.zeros((3, 3, 8, 8, 16, 16), np.float32)
    moved = np.zeros((2, 2, 8, 8, 8, 8), np.float32)
    for p in range(8):
        for q in range(8):
            for e in range(3):
                for f in range(3):
                    j, l = 2 * p - 1 + e, 2 * q - 1 + f
                    if j >= 0 and l >= 0:
                        taps[e, f, q, p, l, rank_of(j)] = 1
            for a in range(2):
                for b in range(2):
                    if q + a < 8 and p + b < 8:
                        moved[a, b, q, p, q + a, p + b] = 1
    return tuple(
        m.astype(BF)
        for m in (
            np.kron(np.eye(8), spread),
            taps.reshape(576, 256),
            moved.reshape(256, 64),
            np.kron(np.eye(16), shift),
            np.kron(np.eye(8), merge),
        )
    )


def place():
    d, s = lax.axis_index("dp"), lax.axis_index("space")
    return d // 2, d % 2, s // (2 * NZ), (s // 2) % NZ, s % 2


def device(xl, core, y, z, xh):
    return {"dp": xl * 2 + core, "space": (y * NZ + z) * 2 + xh}


def remote(src, dst, sems, slot, target):
    copy = pltpu.make_async_remote_copy(
        src_ref=src,
        dst_ref=dst,
        send_sem=sems.at[0, slot],
        recv_sem=sems.at[1, slot],
        device_id=target,
        device_id_type=MESH,
    )
    copy.start()
    return copy


def dot(a, b, ca=1, cb=0):
    return lax.dot_general(a, b, (((ca,), (cb,)), ((), ())), preferred_element_type=F32)


def act_and_slope(v):
    t = jnp.exp(-jnp.abs(v))
    soft = jnp.maximum(v, 0.0) + jnp.log(1.0 + t)
    gate = jnp.where(v >= 0, 1.0, t) / (1.0 + t)
    return 0.2 * v + 0.8 * soft, 0.2 + 0.8 * gate


def far_first(n):
    return sorted(range(1, n), key=lambda k: -min(k, n - k))


class Reduction:
    def __init__(self, s, bufs, sems, peers):
        self.s, self.sems, self.peers = s, sems, peers
        self.r1, self.hy, self.r2, self.hz, self.r3, self.g = bufs
        self.copies = []
        self.slot = 0
        self.at = place()

    def send(self, src, dst, target):
        copy = remote(src, dst, self.sems, self.slot, target)
        self.slot += 1
        self.copies.append(copy)
        return copy

    def cores(self):
        xl, core, y, z, xh = self.at
        self.order = far_first(NY) + [0]
        self.first = {}
        for k in self.order:
            there = (y + k) % NY
            for h in range(2):
                self.first[k, h] = self.send(
                    self.s.at[h * 2 + 1 - core, there, :, pl.ds(0, USED)],
                    self.r1.at[k, h, :, pl.ds(0, USED)],
                    self.peers["core"],
                )

    def plane(self):
        xl, core, y, z, xh = self.at
        self.second = []
        for k in self.order:
            there = (y + k) % NY
            for h in range(2):
                self.first[k, h].wait_recv()
            for h in range(2):
                for v in range(2):
                    left = xl + h - 2 * xl * h
                    half = xh + v - 2 * xh * v
                    for i in range(USED):
                        mine = self.s[left * 2 + core, there, half, i].astype(F32)
                        self.hy[k, h, v, i] = (mine + self.r1[k, left, half, i].astype(F32)).astype(BF)
                    if (k, h, v) != (0, 0, 0):
                        self.second.append(
                            self.send(
                                self.hy.at[k, h, v, pl.ds(0, USED)],
                                self.r2.at[k, h, v, pl.ds(0, USED)],
                                self.peers["plane", k, h, v],
                            )
                        )

    def along_z(self):
        xl, core, y, z, xh = self.at
        for copy in self.second:
            copy.wait_recv()
        self.third = []
        for k in far_first(NZ) + [0]:
            there = (z + k) % NZ
            total = self.hy[0, 0, 0, there].astype(F32)
            for j in range(NY):
                for h in range(2):
                    for v in range(2):
                        if (j, h, v) != (0, 0, 0):
                            total += self.r2[j, h, v, there].astype(F32)
            self.hz[k] = total.astype(BF)
            if k:
                self.third.append(self.send(self.hz.at[k], self.r3.at[k - 1], self.peers["z", k]))

    def gather_z(self):
        xl, core, y, z, xh = self.at
        for copy in self.third:
            copy.wait_recv()
        total = self.hz[0].astype(F32)
        for j in range(NZ - 1):
            total += self.r3[j].astype(F32)
        self.g[y, xh, z] = total.astype(BF)
        self.fifth = {}
        for k in far_first(NZ):
            self.fifth[k] = self.send(self.g.at[y, xh, z], self.g.at[y, xh, z], self.peers["z", k])

    def gather_plane(self):
        xl, core, y, z, xh = self.at
        self.sixth = []
        for k in [0] + sorted(self.fifth, key=lambda k: min(k, NZ - k)):
            if k:
                self.fifth[k].wait_recv()
            part = self.g.at[y, xh, (z + NZ - k) % NZ]
            for j in far_first(NY) + [0]:
                for v in (1, 0):
                    if (j, v) != (0, 0):
                        self.sixth.append(self.send(part, part, self.peers["plane", j, 0, v]))

    def finish(self):
        for copy in self.sixth:
            copy.wait_recv()

    def drain(self):
        for copy in self.copies:
            copy.wait_send()

    @staticmethod
    def scratch(piece):
        blocks = (NY, 2, 2, NZ, piece, 128)
        return [
            pltpu.VMEM((4, NY, 2, NZ, piece, 128), BF),
            pltpu.VMEM(blocks, BF),
            pltpu.VMEM(blocks, BF),
            pltpu.VMEM(blocks, BF),
            pltpu.VMEM((NZ, piece, 128), BF),
            pltpu.VMEM((NZ - 1, piece, 128), BF),
            pltpu.VMEM((NY, 2, NZ, piece, 128), BF),
            pltpu.SemaphoreType.DMA((2, 2 * NY + (4 * NY - 1) + 2 * (NZ - 1) + NZ * (2 * NY - 1))),
        ]


class LineReduction(Reduction):
    def cores(self):
        xl, core, y, z, xh = self.at
        self.first = []
        for h in range(2):
            self.first.append(
                self.send(
                    self.s.at[h * 2 + 1 - core, :, pl.ds(0, USED)], self.r1.at[h, :, pl.ds(0, USED)], self.peers["core"]
                )
            )

    def along_z(self):
        xl, core, y, z, xh = self.at
        for copy in self.first:
            copy.wait_recv()
        self.second = []
        for k in far_first(NZ) + [0]:
            there = (z + k) % NZ
            for h in range(2):
                for i in range(USED):
                    mine = self.s[h * 2 + core, there, i].astype(F32)
                    self.hy[k, h, i] = (mine + self.r1[h, there, i].astype(F32)).astype(BF)
            if k:
                self.second.append(
                    self.send(
                        self.hy.at[k, :, pl.ds(0, USED)], self.r2.at[k - 1, :, pl.ds(0, USED)], self.peers["z", k]
                    )
                )

    def plane(self):
        xl, core, y, z, xh = self.at
        for copy in self.second:
            copy.wait_recv()
        for h in range(2):
            for i in range(USED):
                total = self.hy[0, h, i].astype(F32)
                for j in range(NZ - 1):
                    total += self.r2[j, h, i].astype(F32)
                self.hz[h, i] = total.astype(BF)
            self.hz[h, USED:] = jnp.zeros_like(self.hz[h, USED:])
        self.third = []
        for k in far_first(NY) + [0]:
            for h in range(2):
                for v in range(2):
                    if (k, h, v) != (0, 0, 0):
                        left = xl + h - 2 * xl * h
                        group = (y + k) % NY * 2 + xh + v - 2 * xh * v
                        self.third.append(
                            self.send(self.hz.at[left, group], self.r3.at[k, h, v], self.peers["plane", k, h, v])
                        )

    def gather_plane(self):
        xl, core, y, z, xh = self.at
        for copy in self.third:
            copy.wait_recv()
        mine = y * 2 + xh
        total = self.hz[xl, mine].astype(F32)
        for k in range(NY):
            for h in range(2):
                for v in range(2):
                    if (k, h, v) != (0, 0, 0):
                        total += self.r3[k, h, v].astype(F32)
        self.g[z, mine] = total.astype(BF)
        self.fifth = []
        for k in far_first(NY) + [0]:
            for v in (1, 0):
                if (k, v) != (0, 0):
                    self.fifth.append(self.send(self.g.at[z, mine], self.g.at[z, mine], self.peers["plane", k, 0, v]))

    def gather_z(self):
        xl, core, y, z, xh = self.at
        for copy in self.fifth:
            copy.wait_recv()
        self.sixth = []
        part = self.g.at[z, pl.ds(0, USED)]
        for k in far_first(NZ):
            self.sixth.append(self.send(part, part, self.peers["z", k]))

    @staticmethod
    def scratch(piece):
        return [
            pltpu.VMEM((4, NZ, 2 * NY, piece, 128), BF),
            pltpu.VMEM((2, NZ, 2 * NY, piece, 128), BF),
            pltpu.VMEM((NZ, 2, 2 * NY, piece, 128), BF),
            pltpu.VMEM((NZ - 1, 2, 2 * NY, piece, 128), BF),
            pltpu.VMEM((2, 2 * NY, piece, 128), BF),
            pltpu.VMEM((NY, 2, 2, piece, 128), BF),
            pltpu.VMEM((NZ, 2 * NY, piece, 128), BF),
            pltpu.SemaphoreType.DMA((2, 2 + 2 * (NZ - 1) + (4 * NY - 1) + (2 * NY - 1))),
        ]


def step_kernel(scales, vol, w1, w2, cot, p0, p1, p2, p3, p4, actv, ig, g1out, g2out, *scratch):
    xe, xhalo, w1g, w1p, wb, w2g, hid, hhalo, slope, l2, d2, d2e, d1e, un = scratch[:14]
    wsem, hsem = scratch[14:16]
    s1, *bufs1, sems1 = scratch[16:24]
    s2, *bufs2, sems2 = scratch[24:32]
    at = xl, core, y, z, xh = place()
    s, d = lax.axis_index("space"), lax.axis_index("dp")
    n = 2 * NY * NZ
    bottom, top = s == 0, s == n - 1
    upper = {"space": (s + 1) % n}
    lower = {"space": (s + n - 1) % n}
    peers = {"core": device(xl, 1 - core, y, z, xh)}
    for k in range(NY):
        for h in range(2):
            for v in range(2):
                if (k, h, v) != (0, 0, 0):
                    there = xl + h - 2 * xl * h, core, (y + k) % NY, z, xh + v - 2 * xh * v
                    peers["plane", k, h, v] = device(*there)
    for k in range(1, NZ):
        peers["z", k] = device(xl, core, y, (z + k) % NZ, xh)
    peers["upper"], peers["lower"] = upper, lower

    barrier = pltpu.get_barrier_semaphore()
    for peer in peers.values():
        pl.semaphore_signal(barrier, inc=1, device_id=peer, device_id_type=MESH)
    pl.semaphore_wait(barrier, len(peers))

    def rows(q, size, lo, hi):
        return pl.ds(pl.multiple_of(q * size + lo, 16), hi - lo)

    sent = []
    forward = []
    theirs = (1 - xl) * 2 + core
    for slot, (own, whole, size, cut) in enumerate(((w1, w1g, 432, 224), (w2, w2g, 864, 432))):
        base = slot * 5
        parts = ((0, cut, peers["plane", 0, 1, 0]), (cut, size, peers["plane", 0, 1, 1]))
        arriving = []
        for j, (lo, hi, peer) in enumerate(parts):
            arriving.append(remote(own.at[pl.ds(lo, hi - lo)], whole.at[rows(d, size, lo, hi)], wsem, base + j, peer))
        to_core = remote(own, whole.at[rows(d, size, 0, size)], wsem, base + 2, peers["core"])
        forward.append((whole, size, parts, arriving, to_core, base))
        sent += arriving + [to_core]
        if slot == 0:
            halo_in = remote(vol.at[pl.ds(224, 32)], xhalo, hsem, 0, upper)

    passed = []

    def pass_on(slot):
        whole, size, parts, arriving, to_core, base = forward[slot]
        for j, (lo, hi, _) in enumerate(parts):
            arriving[j].wait_recv()
            part = whole.at[rows(theirs, size, lo, hi)]
            passed.append(remote(part, part, wsem, base + 3 + j, peers["core"]))
        return to_core, passed[-2:]

    xe[:, :, 0] = jnp.zeros((9, 3, 16, 128), BF)

    @pl.loop(0, 8)
    def _(c):
        got = dot(p0[...], vol[:, pl.ds(pl.multiple_of(c * 256, 256), 256)]).astype(BF)
        for i in range(8):
            for e in range(3):
                for u in range(2):
                    xe[i + 1, e, 2 * c + 1 + u] = got[(i * 3 + e) * 16 : (i * 3 + e + 1) * 16, u * 128 : (u + 1) * 128]

    w1g[rows(d, 432, 0, 432)] = w1[...]
    w2g[rows(d, 864, 0, 864)] = w2[...]
    to_core, others = pass_on(0)
    to_core.wait_recv()
    for copy in others:
        copy.wait_recv()
    for t in range(9):
        w1p[t * 256 : t * 256 + 64] = jnp.zeros((64, 128), BF)
        w1p[t * 256 + 64 : t * 256 + 256] = w1g[t * 192 : (t + 1) * 192]

    def conv_first(o):
        tiles = []
        for a in range(3):
            for e in range(3):
                tiles.append(xe[2 * o + a, e, 0:16].reshape(256, 128))
                tiles.append(xe[2 * o + a, e, 1:17].reshape(256, 128))
        value, gate = act_and_slope(dot(jnp.concatenate(tiles, axis=1), w1p[...]))
        hid[o] = value.astype(BF)
        slope[o] = gate.reshape(16, 16, 128)

    conv_first(3)
    halo_hid = remote(hid.at[3], hhalo, hsem, 1, upper)
    to_core_second, others_second = pass_on(1)

    @pl.loop(1, 3)
    def _(o):
        conv_first(o)

    halo_in.wait_recv()
    rim = jnp.where(bottom, jnp.zeros_like(xhalo), xhalo[...])
    got = dot(p0[0:48, 0:32], rim).astype(BF)
    for e in range(3):
        for u in range(16):
            xe[0, e, u + 1] = got[e * 16 : (e + 1) * 16, u * 128 : (u + 1) * 128]
    conv_first(0)

    def place_taps(got, plane):
        for o in range(2):
            a = plane - 2 * o
            if 0 <= a < 3:
                for k in range(9):
                    l2[o * 64 : (o + 1) * 64, (a * 9 + k) * 128 : (a * 9 + k + 1) * 128] = got[k * 64 : (k + 1) * 64]

    for pair in range(2):
        both = jnp.concatenate([hid[2 * pair], hid[2 * pair + 1]], axis=1)
        got = dot(p1[...], both).astype(BF)
        place_taps(got[:, :128], 2 * pair + 1)
        place_taps(got[:, 128:], 2 * pair + 2)
    for t in range(9):
        block = w1p[t * 256 : (t + 1) * 256]
        wb[t * 256 : t * 256 + 128] = block[128:].T
        wb[t * 256 + 128 : (t + 1) * 256] = block[:128].T
    halo_hid.wait_recv()
    rim = jnp.where(bottom, jnp.zeros_like(hhalo), hhalo[...])
    place_taps(dot(p1[...], rim).astype(BF), 0)
    to_core_second.wait_recv()
    for copy in others_second:
        copy.wait_recv()

    linear = dot(l2[...], w2g[...])
    value, gate = act_and_slope(linear)
    arriving = jnp.concatenate(
        [cot[o, :, q * 256 : (q + 1) * 256].astype(F32) for o in range(2) for q in range(8)], axis=0
    )
    delta = (arriving * gate).astype(BF)
    d2[0] = delta[:64]
    halo_d2 = remote(d2.at[0], d2.at[2], hsem, 2, lower)
    d2[1] = delta[64:]
    for o in range(2):
        for q in range(8):
            at_row = (o * 8 + q) * 8
            actv[o, :, q * 256 : (q + 1) * 256] = value[at_row : at_row + 8].astype(BF)

    def pieces(lo, hi, group, piece):
        while lo < hi:
            where = lo % group
            count = min(hi - lo, group - where, piece - where % piece)
            yield lo, count, lo // group, where // piece, where % piece
            lo += count

    for t in range(27):
        got = dot(l2[:, t * 128 : (t + 1) * 128], delta, 0, 0)
        for q in range(4):
            lo, hi = max(t * 128, q * 864), min(t * 128 + 128, q * 864 + 864)
            for row, count, g, k, at_row in pieces(lo - q * 864, hi - q * 864, GROUP2, PIECE2):
                row += q * 864 - t * 128
                for half in range(2):
                    block = got[row : row + count, half * 128 : (half + 1) * 128].astype(BF)
                    h = half * NY + g
                    s2[q, h // 2, h % 2, k, at_row : at_row + count] = block
    sum2 = Reduction(s2, bufs2, sems2, peers)
    sum1 = LineReduction(s1, bufs1, sems1, peers)
    sum2.cores()

    def spread_delta(o):
        got = dot(p2[...], d2[o]).astype(BF)
        for v in range(4):
            d2e[o, v] = got[v * 64 : (v + 1) * 64]

    taps_of = (((1, 0),), ((2, 0), (0, 1)))

    def hidden_delta(pi):
        for pq in range(2):
            halves = []
            for pj in range(2):
                left, right = [], []
                for a, sa in taps_of[pi]:
                    for e, se in taps_of[pj]:
                        for f, sf in taps_of[pq]:
                            left.append(d2e[sa : sa + 2, sf * 2 + se].reshape(128, 256))
                            t = a * 9 + e * 3 + f
                            right.append(w2g[t * 128 : (t + 1) * 128])
                got = dot(jnp.concatenate(left, axis=1), jnp.concatenate(right, axis=1), 1, 1)
                halves.append(got.reshape(2, 8, 8, 128))
            both = jnp.concatenate(halves, axis=2)
            for i in range(2):
                for q in range(8):
                    d1e[2 * i + pi, 0, 2 * q + pq] = (both[i, q] * slope[2 * i + pi, 2 * q + pq]).astype(BF)

    spread_delta(0)
    spread_delta(1)
    d1e[:, :, 16] = jnp.zeros((5, 2, 16, 128), BF)
    hidden_delta(0)
    halo_d1 = remote(d1e.at[0, 0, pl.ds(0, 16)], d1e.at[4, 0, pl.ds(0, 16)], hsem, 3, lower)
    sum2.plane()
    halo_d2.wait_recv()
    d2[2] = jnp.where(top, jnp.zeros((64, 256), BF), d2[2])
    spread_delta(2)
    hidden_delta(1)

    flat1 = jnp.concatenate([d1e[o, 0, 0:16].reshape(256, 128) for o in range(4)], axis=0)

    @pl.loop(0, 9)
    def _(t):
        a, e = t // 3, t % 3
        left = jnp.concatenate(
            [
                jnp.concatenate(
                    [xe[2 * o + a, e, 0:16].reshape(256, 128), xe[2 * o + a, e, 1:17].reshape(256, 128)], axis=1
                )
                for o in range(4)
            ],
            axis=0,
        )
        got = dot(left, flat1, 0, 0)
        for k in range(24):
            block = t * 24 + k
            g = block % 54 // 7
            s1[block // 54, g, block % 54 % 7] = got[64 + k * 8 : 64 + (k + 1) * 8].astype(BF)

    sum1.cores()

    def shift_delta(first, count):
        both = jnp.concatenate([d1e[first + k, 0, 0:16].reshape(256, 128) for k in range(count)], axis=1)
        got = dot(p3[...], both).astype(BF)
        for k in range(count):
            d1e[first + k, 1, 0:16] = got[:, k * 128 : (k + 1) * 128].reshape(16, 16, 128)

    def input_delta(pi, pj):
        @pl.loop(0, 4)
        def _(i):
            left, right = [], []
            for a, sa in taps_of[pi]:
                for e, se in taps_of[pj]:
                    left.append(d1e[i + sa, se, 0:16].reshape(256, 128))
                    left.append(d1e[i + sa, se, 1:17].reshape(256, 128))
                    t = a * 3 + e
                    right.append(wb[t * 256 : (t + 1) * 256])
            got = dot(jnp.concatenate(left, axis=1), jnp.concatenate(right, axis=0)).astype(BF)
            for q in range(16):
                un[2 * i + pi, pj * 16 : (pj + 1) * 16, q * 128 : (q + 1) * 128] = got[q * 16 : (q + 1) * 16]

    shift_delta(0, 2)
    shift_delta(2, 2)
    input_delta(0, 0)
    sum1.along_z()
    input_delta(0, 1)
    halo_d1.wait_recv()
    d1e[4, 0, 0:16] = jnp.where(top, jnp.zeros((16, 16, 128), BF), d1e[4, 0, 0:16])
    shift_delta(4, 1)
    input_delta(1, 0)
    input_delta(1, 1)

    @pl.loop(0, 8)
    def _(c):
        lanes = pl.ds(pl.multiple_of(c * 256, 256), 256)
        ig[:, lanes] = dot(p4[...], un[:, :, lanes].reshape(256, 256)).astype(BF)

    sum2.along_z()
    sum1.plane()
    sum2.gather_z()
    sum1.gather_plane()
    sum2.gather_plane()
    sum1.gather_z()
    sum2.finish()
    whole = bufs2[-1]
    for row, count, g, k, at_row in pieces(0, 1728, GROUP2, PIECE2):
        got = whole[g // 2, g % 2, k, at_row : at_row + count].astype(F32) * scales[1]
        half = row // 864
        g2out[row % 864 : row % 864 + count, half * 128 : (half + 1) * 128] = got
    sum1.finish()
    whole = bufs1[-1]
    for row, count, g, k, at_row in pieces(0, 432, GROUP1, PIECE1):
        g1out[row : row + count] = whole[g, k].astype(F32) * scales[0]

    for copy in sent + passed + [halo_in, halo_hid, halo_d2, halo_d1]:
        copy.wait_send()
    sum2.drain()
    sum1.drain()


def local(volume, weight_first, weight_second, cotangent):
    cells = 4 * lax.axis_size("space") * 4 * 256
    scales = (float(cells) ** -0.5, float(cells // 8) ** -0.5)
    vmem = pl.BlockSpec(memory_space=pltpu.VMEM)
    shape = jax.ShapeDtypeStruct

    def body(*refs):
        step_kernel(scales, *refs)

    activations, input_gradient, first, second = pl.pallas_call(
        body,
        out_shape=(
            shape((2, 8, 2048), BF),
            shape((256, 2048), BF),
            shape((432, 128), F32),
            shape((864, 256), F32),
        ),
        in_specs=[vmem] * 9,
        out_specs=(vmem,) * 4,
        scratch_shapes=[
            pltpu.VMEM((9, 3, 17, 16, 128), BF),
            pltpu.VMEM((32, 2048), BF),
            pltpu.VMEM((1728, 128), BF),
            pltpu.VMEM((2304, 128), BF),
            pltpu.VMEM((2304, 128), BF),
            pltpu.VMEM((3456, 256), BF),
            pltpu.VMEM((4, 256, 128), BF),
            pltpu.VMEM((256, 128), BF),
            pltpu.VMEM((4, 16, 16, 128), F32),
            pltpu.VMEM((128, 3456), BF),
            pltpu.VMEM((3, 64, 256), BF),
            pltpu.VMEM((3, 4, 64, 256), BF),
            pltpu.VMEM((5, 2, 17, 16, 128), BF),
            pltpu.VMEM((8, 32, 2048), BF),
            pltpu.SemaphoreType.DMA((2, 10)),
            pltpu.SemaphoreType.DMA((2, 4)),
        ]
        + LineReduction.scratch(PIECE1)
        + Reduction.scratch(PIECE2),
        compiler_params=pltpu.CompilerParams(
            collective_id=0, has_side_effects=True, vmem_limit_bytes=60 * 1024 * 1024
        ),
        name="step",
    )(
        volume.reshape(256, 2048),
        weight_first,
        weight_second,
        cotangent.reshape(2, 8, 2048),
        *selections(),
    )
    return (
        activations.reshape(cotangent.shape),
        input_gradient.reshape(volume.shape),
        first,
        second,
    )


def solution(mesh):
    return jax.shard_map(
        local,
        mesh=mesh,
        in_specs=(
            P("dp", "space", None, None),
            P("dp", None),
            P("dp", None),
            P("dp", "space", None, None),
        ),
        out_specs=(
            P("dp", "space", None, None),
            P("dp", "space", None, None),
            P("dp", None),
            P("dp", None),
        ),
        check_vma=False,
    )
```

```python
import numpy as np

import jax
import jax.numpy as jnp
from jax import lax
from jax.experimental import pallas as pl
from jax.experimental.pallas import tpu as pltpu
from jax.sharding import PartitionSpec as P

NY, NZ = 4, 8
BF, F32 = jnp.bfloat16, jnp.float32
PIECE1, PIECE2 = 8, 32
GROUP1, GROUP2 = 56, 216
VLIM = 40
OUT = pltpu.VMEM
USED = 7
MESH = pl.DeviceIdType.MESH


def rank_of(p):
    return (p % 2) * 8 + p // 2


def selections():
    spread = np.zeros((48, 32), np.float32)
    shift = np.zeros((16, 16), np.float32)
    merge = np.zeros((32, 32), np.float32)
    for p in range(16):
        for e in range(3):
            if 2 * p - 1 + e >= 0:
                spread[e * 16 + rank_of(p), 2 * p - 1 + e] = 1
        if p < 15:
            shift[rank_of(p), rank_of(p + 1)] = 1
        for parity in range(2):
            merge[2 * p + parity, parity * 16 + rank_of(p)] = 1
    taps = np.zeros((3, 3, 8, 8, 16, 16), np.float32)
    moved = np.zeros((2, 2, 8, 8, 8, 8), np.float32)
    for p in range(8):
        for q in range(8):
            for e in range(3):
                for f in range(3):
                    j, l = 2 * p - 1 + e, 2 * q - 1 + f
                    if j >= 0 and l >= 0:
                        taps[e, f, q, p, l, rank_of(j)] = 1
            for a in range(2):
                for b in range(2):
                    if q + a < 8 and p + b < 8:
                        moved[a, b, q, p, q + a, p + b] = 1
    return tuple(
        m.astype(BF)
        for m in (
            np.kron(np.eye(8), spread),
            taps.reshape(576, 256),
            moved.reshape(256, 64),
            np.kron(np.eye(16), shift),
            np.kron(np.eye(8), merge),
        )
    )


def place():
    d, s = lax.axis_index("dp"), lax.axis_index("space")
    return d // 2, d % 2, s // (2 * NZ), (s // 2) % NZ, s % 2


def device(xl, core, y, z, xh):
    return {"dp": xl * 2 + core, "space": (y * NZ + z) * 2 + xh}


def remote(src, dst, sems, slot, target):
    copy = pltpu.make_async_remote_copy(
        src_ref=src,
        dst_ref=dst,
        send_sem=sems.at[0, slot],
        recv_sem=sems.at[1, slot],
        device_id=target,
        device_id_type=MESH,
    )
    copy.start()
    return copy


def dot(a, b, ca=1, cb=0):
    return lax.dot_general(a, b, (((ca,), (cb,)), ((), ())), preferred_element_type=F32)


def act_and_slope(v):
    t = jnp.exp(-jnp.abs(v))
    soft = jnp.maximum(v, 0.0) + jnp.log(1.0 + t)
    gate = jnp.where(v >= 0, 1.0, t) / (1.0 + t)
    return 0.2 * v + 0.8 * soft, 0.2 + 0.8 * gate


def far_first(n):
    return sorted(range(1, n), key=lambda k: -min(k, n - k))


class Reduction:
    def __init__(self, s, bufs, sems, peers):
        self.s, self.sems, self.peers = s, sems, peers
        self.r1, self.hy, self.r2, self.hz, self.r3, self.g = bufs
        self.copies = []
        self.slot = 0
        self.at = place()

    def send(self, src, dst, target):
        copy = remote(src, dst, self.sems, self.slot, target)
        self.slot += 1
        self.copies.append(copy)
        return copy

    def cores(self):
        xl, core, y, z, xh = self.at
        self.order = far_first(NY) + [0]
        self.first = {}
        for k in self.order:
            there = (y + k) % NY
            for h in range(2):
                self.first[k, h] = self.send(
                    self.s.at[h * 2 + 1 - core, there, :, pl.ds(0, USED)],
                    self.r1.at[k, h, :, pl.ds(0, USED)],
                    self.peers["core"],
                )

    def plane(self):
        xl, core, y, z, xh = self.at
        self.second = []
        for k in self.order:
            there = (y + k) % NY
            for h in range(2):
                self.first[k, h].wait_recv()
            for h in range(2):
                for v in range(2):
                    left = xl + h - 2 * xl * h
                    half = xh + v - 2 * xh * v
                    for i in range(USED):
                        mine = self.s[left * 2 + core, there, half, i].astype(F32)
                        self.hy[k, h, v, i] = (mine + self.r1[k, left, half, i].astype(F32)).astype(BF)
                    if (k, h, v) != (0, 0, 0):
                        self.second.append(
                            self.send(
                                self.hy.at[k, h, v, pl.ds(0, USED)],
                                self.r2.at[k, h, v, pl.ds(0, USED)],
                                self.peers["plane", k, h, v],
                            )
                        )

    def along_z(self):
        xl, core, y, z, xh = self.at
        for copy in self.second:
            copy.wait_recv()
        self.third = []
        for k in far_first(NZ) + [0]:
            there = (z + k) % NZ
            total = self.hy[0, 0, 0, there].astype(F32)
            for j in range(NY):
                for h in range(2):
                    for v in range(2):
                        if (j, h, v) != (0, 0, 0):
                            total += self.r2[j, h, v, there].astype(F32)
            self.hz[k] = total.astype(BF)
            if k:
                self.third.append(self.send(self.hz.at[k], self.r3.at[k - 1], self.peers["z", k]))

    def gather_z(self):
        xl, core, y, z, xh = self.at
        for copy in self.third:
            copy.wait_recv()
        total = self.hz[0].astype(F32)
        for j in range(NZ - 1):
            total += self.r3[j].astype(F32)
        self.g[y, xh, z] = total.astype(BF)
        self.fifth = {}
        for k in far_first(NZ):
            self.fifth[k] = self.send(self.g.at[y, xh, z], self.g.at[y, xh, z], self.peers["z", k])

    def gather_plane(self):
        xl, core, y, z, xh = self.at
        self.sixth = []
        for k in [0] + sorted(self.fifth, key=lambda k: min(k, NZ - k)):
            if k:
                self.fifth[k].wait_recv()
            part = self.g.at[y, xh, (z + NZ - k) % NZ]
            for j in far_first(NY) + [0]:
                for v in (1, 0):
                    if (j, v) != (0, 0):
                        self.sixth.append(self.send(part, part, self.peers["plane", j, 0, v]))

    def finish(self):
        for copy in self.sixth:
            copy.wait_recv()

    def drain(self):
        for copy in self.copies:
            copy.wait_send()

    @staticmethod
    def scratch(piece):
        blocks = (NY, 2, 2, NZ, piece, 128)
        return [
            pltpu.VMEM((4, NY, 2, NZ, piece, 128), BF),
            pltpu.VMEM(blocks, BF),
            pltpu.VMEM(blocks, BF),
            pltpu.VMEM(blocks, BF),
            pltpu.VMEM((NZ, piece, 128), BF),
            pltpu.VMEM((NZ - 1, piece, 128), BF),
            pltpu.SemaphoreType.DMA((2, 2 * NY + (4 * NY - 1) + 2 * (NZ - 1) + NZ * (2 * NY - 1))),
        ]


class LineReduction(Reduction):
    def cores(self):
        xl, core, y, z, xh = self.at
        self.first = []
        for h in range(2):
            self.first.append(
                self.send(
                    self.s.at[h * 2 + 1 - core, :, pl.ds(0, USED)], self.r1.at[h, :, pl.ds(0, USED)], self.peers["core"]
                )
            )

    def along_z(self):
        xl, core, y, z, xh = self.at
        for copy in self.first:
            copy.wait_recv()
        self.second = []
        for k in far_first(NZ) + [0]:
            there = (z + k) % NZ
            for h in range(2):
                for i in range(USED):
                    mine = self.s[h * 2 + core, there, i].astype(F32)
                    self.hy[k, h, i] = (mine + self.r1[h, there, i].astype(F32)).astype(BF)
            if k:
                self.second.append(
                    self.send(
                        self.hy.at[k, :, pl.ds(0, USED)], self.r2.at[k - 1, :, pl.ds(0, USED)], self.peers["z", k]
                    )
                )

    def plane(self):
        xl, core, y, z, xh = self.at
        for copy in self.second:
            copy.wait_recv()
        for h in range(2):
            for i in range(USED):
                total = self.hy[0, h, i].astype(F32)
                for j in range(NZ - 1):
                    total += self.r2[j, h, i].astype(F32)
                self.hz[h, i] = total.astype(BF)
            self.hz[h, USED:] = jnp.zeros_like(self.hz[h, USED:])
        self.third = []
        for k in far_first(NY) + [0]:
            for h in range(2):
                for v in range(2):
                    if (k, h, v) != (0, 0, 0):
                        left = xl + h - 2 * xl * h
                        group = (y + k) % NY * 2 + xh + v - 2 * xh * v
                        self.third.append(
                            self.send(self.hz.at[left, group], self.r3.at[k, h, v], self.peers["plane", k, h, v])
                        )

    def gather_plane(self):
        xl, core, y, z, xh = self.at
        for copy in self.third:
            copy.wait_recv()
        mine = y * 2 + xh
        total = self.hz[xl, mine].astype(F32)
        for k in range(NY):
            for h in range(2):
                for v in range(2):
                    if (k, h, v) != (0, 0, 0):
                        total += self.r3[k, h, v].astype(F32)
        self.g[z, mine] = total.astype(BF)
        self.fifth = []
        for k in far_first(NY) + [0]:
            for v in (1, 0):
                if (k, v) != (0, 0):
                    self.fifth.append(self.send(self.g.at[z, mine], self.g.at[z, mine], self.peers["plane", k, 0, v]))

    def gather_z(self):
        xl, core, y, z, xh = self.at
        for copy in self.fifth:
            copy.wait_recv()
        self.sixth = []
        part = self.g.at[z, pl.ds(0, USED)]
        for k in far_first(NZ):
            self.sixth.append(self.send(part, part, self.peers["z", k]))

    @staticmethod
    def scratch(piece):
        return [
            pltpu.VMEM((4, NZ, 2 * NY, piece, 128), BF),
            pltpu.VMEM((2, NZ, 2 * NY, piece, 128), BF),
            pltpu.VMEM((NZ, 2, 2 * NY, piece, 128), BF),
            pltpu.VMEM((NZ - 1, 2, 2 * NY, piece, 128), BF),
            pltpu.VMEM((2, 2 * NY, piece, 128), BF),
            pltpu.VMEM((NY, 2, 2, piece, 128), BF),
            pltpu.SemaphoreType.DMA((2, 2 + 2 * (NZ - 1) + (4 * NY - 1) + (2 * NY - 1))),
        ]


def pieces(lo, hi, group, piece):
    while lo < hi:
        where = lo % group
        count = min(hi - lo, group - where, piece - where % piece)
        yield lo, count, lo // group, where // piece, where % piece
        lo += count


def finish_kernel(scales, actv, ig, g1, g2, actv_out, ig_out, g1out, g2out, sems):
    copies = [pltpu.make_async_copy(ig, ig_out, sems.at[0]), pltpu.make_async_copy(actv, actv_out, sems.at[1])]
    for copy in copies:
        copy.start()
    for row, count, g, k, at_row in pieces(0, 1728, GROUP2, PIECE2):
        got = g2[g // 2, g % 2, k, at_row : at_row + count].astype(F32) * scales[1]
        half = row // 864
        g2out[row % 864 : row % 864 + count, half * 128 : (half + 1) * 128] = got
    for row, count, g, k, at_row in pieces(0, 432, GROUP1, PIECE1):
        g1out[row : row + count] = g1[g, k].astype(F32) * scales[0]
    for copy in copies:
        copy.wait()


def step_kernel(vol_in, w1, w2, cot_in, p0_in, p1_in, p2_in, p3_in, p4_in, actv, ig, g1, g2, *scratch):
    vol, cot, p0, p1, p2, p3, p4, lsem = scratch[30:]
    loads = []
    for k, (src, dst) in enumerate(
        ((vol_in, vol), (p0_in, p0), (p1_in, p1), (cot_in, cot), (p2_in, p2), (p3_in, p3), (p4_in, p4))
    ):
        loads.append(pltpu.make_async_copy(src, dst, lsem.at[k]))
        loads[-1].start()
    xe, xhalo, w1g, w1p, wb, w2g, hid, hhalo, slope, l2, d2, d2e, d1e, un = scratch[:14]
    wsem, hsem = scratch[14:16]
    s1, *bufs1, sems1 = scratch[16:23]
    s2, *bufs2, sems2 = scratch[23:30]
    bufs1.append(g1)
    bufs2.append(g2)
    at = xl, core, y, z, xh = place()
    s, d = lax.axis_index("space"), lax.axis_index("dp")
    n = 2 * NY * NZ
    bottom, top = s == 0, s == n - 1
    upper = {"space": (s + 1) % n}
    lower = {"space": (s + n - 1) % n}
    peers = {"core": device(xl, 1 - core, y, z, xh)}
    for k in range(NY):
        for h in range(2):
            for v in range(2):
                if (k, h, v) != (0, 0, 0):
                    there = xl + h - 2 * xl * h, core, (y + k) % NY, z, xh + v - 2 * xh * v
                    peers["plane", k, h, v] = device(*there)
    for k in range(1, NZ):
        peers["z", k] = device(xl, core, y, (z + k) % NZ, xh)
    peers["upper"], peers["lower"] = upper, lower

    held = []
    for k, (src, dst, size) in enumerate(((w1, w1g, 432), (w2, w2g, 864))):
        at_rows = pl.ds(pl.multiple_of(d * size, 16), size)
        held.append(pltpu.make_async_copy(src, dst.at[at_rows], lsem.at[7 + k]))
        held[-1].start()

    barrier = pltpu.get_barrier_semaphore()
    for peer in peers.values():
        pl.semaphore_signal(barrier, inc=1, device_id=peer, device_id_type=MESH)
    pl.semaphore_wait(barrier, len(peers))

    def rows(q, size, lo, hi):
        return pl.ds(pl.multiple_of(q * size + lo, 16), hi - lo)

    sent = []
    forward = []
    theirs = (1 - xl) * 2 + core
    for slot, (own, whole, size, cut) in enumerate(((w1, w1g, 432, 224), (w2, w2g, 864, 432))):
        base = slot * 5
        parts = ((0, cut, peers["plane", 0, 1, 0]), (cut, size, peers["plane", 0, 1, 1]))
        arriving = []
        for j, (lo, hi, peer) in enumerate(parts):
            arriving.append(remote(own.at[pl.ds(lo, hi - lo)], whole.at[rows(d, size, lo, hi)], wsem, base + j, peer))
        to_core = remote(own, whole.at[rows(d, size, 0, size)], wsem, base + 2, peers["core"])
        forward.append((whole, size, parts, arriving, to_core, base))
        sent += arriving + [to_core]
        if slot == 0:
            halo_in = remote(vol_in.at[pl.ds(224, 32)], xhalo, hsem, 0, upper)

    passed = []

    def pass_on(slot):
        whole, size, parts, arriving, to_core, base = forward[slot]
        for j, (lo, hi, _) in enumerate(parts):
            arriving[j].wait_recv()
            part = whole.at[rows(theirs, size, lo, hi)]
            passed.append(remote(part, part, wsem, base + 3 + j, peers["core"]))
        return to_core, passed[-2:]

    xe[:, :, 0] = jnp.zeros((9, 3, 16, 128), BF)
    for copy in loads + held:
        copy.wait()

    @pl.loop(0, 8)
    def _(c):
        got = dot(p0[...], vol[:, pl.ds(pl.multiple_of(c * 256, 256), 256)]).astype(BF)
        for i in range(8):
            for e in range(3):
                for u in range(2):
                    xe[i + 1, e, 2 * c + 1 + u] = got[(i * 3 + e) * 16 : (i * 3 + e + 1) * 16, u * 128 : (u + 1) * 128]

    to_core, others = pass_on(0)
    to_core.wait_recv()
    for copy in others:
        copy.wait_recv()
    for t in range(9):
        w1p[t * 256 : t * 256 + 64] = jnp.zeros((64, 128), BF)
        w1p[t * 256 + 64 : t * 256 + 256] = w1g[t * 192 : (t + 1) * 192]

    def conv_first(o):
        tiles = []
        for a in range(3):
            for e in range(3):
                tiles.append(xe[2 * o + a, e, 0:16].reshape(256, 128))
                tiles.append(xe[2 * o + a, e, 1:17].reshape(256, 128))
        value, gate = act_and_slope(dot(jnp.concatenate(tiles, axis=1), w1p[...]))
        hid[o] = value.astype(BF)
        slope[o] = gate.reshape(16, 16, 128)

    conv_first(3)
    halo_hid = remote(hid.at[3], hhalo, hsem, 1, upper)
    to_core_second, others_second = pass_on(1)

    @pl.loop(1, 3)
    def _(o):
        conv_first(o)

    halo_in.wait_recv()
    rim = jnp.where(bottom, jnp.zeros_like(xhalo), xhalo[...])
    got = dot(p0[0:48, 0:32], rim).astype(BF)
    for e in range(3):
        for u in range(16):
            xe[0, e, u + 1] = got[e * 16 : (e + 1) * 16, u * 128 : (u + 1) * 128]
    conv_first(0)

    def place_taps(got, plane):
        for o in range(2):
            a = plane - 2 * o
            if 0 <= a < 3:
                for k in range(9):
                    l2[o * 64 : (o + 1) * 64, (a * 9 + k) * 128 : (a * 9 + k + 1) * 128] = got[k * 64 : (k + 1) * 64]

    for pair in range(2):
        both = jnp.concatenate([hid[2 * pair], hid[2 * pair + 1]], axis=1)
        got = dot(p1[...], both).astype(BF)
        place_taps(got[:, :128], 2 * pair + 1)
        place_taps(got[:, 128:], 2 * pair + 2)
    for t in range(9):
        block = w1p[t * 256 : (t + 1) * 256]
        wb[t * 256 : t * 256 + 128] = block[128:].T
        wb[t * 256 + 128 : (t + 1) * 256] = block[:128].T
    halo_hid.wait_recv()
    rim = jnp.where(bottom, jnp.zeros_like(hhalo), hhalo[...])
    place_taps(dot(p1[...], rim).astype(BF), 0)
    to_core_second.wait_recv()
    for copy in others_second:
        copy.wait_recv()

    linear = dot(l2[...], w2g[...])
    value, gate = act_and_slope(linear)
    arriving = jnp.concatenate(
        [cot[o, :, q * 256 : (q + 1) * 256].astype(F32) for o in range(2) for q in range(8)], axis=0
    )
    delta = (arriving * gate).astype(BF)
    d2[0] = delta[:64]
    halo_d2 = remote(d2.at[0], d2.at[2], hsem, 2, lower)
    d2[1] = delta[64:]
    for o in range(2):
        for q in range(8):
            at_row = (o * 8 + q) * 8
            actv[o, :, q * 256 : (q + 1) * 256] = value[at_row : at_row + 8].astype(BF)

    for t in range(27):
        got = dot(l2[:, t * 128 : (t + 1) * 128], delta, 0, 0)
        for q in range(4):
            lo, hi = max(t * 128, q * 864), min(t * 128 + 128, q * 864 + 864)
            for row, count, g, k, at_row in pieces(lo - q * 864, hi - q * 864, GROUP2, PIECE2):
                row += q * 864 - t * 128
                for half in range(2):
                    block = got[row : row + count, half * 128 : (half + 1) * 128].astype(BF)
                    h = half * NY + g
                    s2[q, h // 2, h % 2, k, at_row : at_row + count] = block
    sum2 = Reduction(s2, bufs2, sems2, peers)
    sum1 = LineReduction(s1, bufs1, sems1, peers)
    sum2.cores()

    def spread_delta(o):
        got = dot(p2[...], d2[o]).astype(BF)
        for v in range(4):
            d2e[o, v] = got[v * 64 : (v + 1) * 64]

    taps_of = (((1, 0),), ((2, 0), (0, 1)))

    def hidden_delta(pi):
        for pq in range(2):
            halves = []
            for pj in range(2):
                left, right = [], []
                for a, sa in taps_of[pi]:
                    for e, se in taps_of[pj]:
                        for f, sf in taps_of[pq]:
                            left.append(d2e[sa : sa + 2, sf * 2 + se].reshape(128, 256))
                            t = a * 9 + e * 3 + f
                            right.append(w2g[t * 128 : (t + 1) * 128])
                got = dot(jnp.concatenate(left, axis=1), jnp.concatenate(right, axis=1), 1, 1)
                halves.append(got.reshape(2, 8, 8, 128))
            both = jnp.concatenate(halves, axis=2)
            for i in range(2):
                for q in range(8):
                    d1e[2 * i + pi, 0, 2 * q + pq] = (both[i, q] * slope[2 * i + pi, 2 * q + pq]).astype(BF)

    spread_delta(0)
    spread_delta(1)
    d1e[:, :, 16] = jnp.zeros((5, 2, 16, 128), BF)
    hidden_delta(0)
    halo_d1 = remote(d1e.at[0, 0, pl.ds(0, 16)], d1e.at[4, 0, pl.ds(0, 16)], hsem, 3, lower)
    sum2.plane()
    halo_d2.wait_recv()
    d2[2] = jnp.where(top, jnp.zeros((64, 256), BF), d2[2])
    spread_delta(2)
    hidden_delta(1)

    flat1 = jnp.concatenate([d1e[o, 0, 0:16].reshape(256, 128) for o in range(4)], axis=0)

    @pl.loop(0, 9)
    def _(t):
        a, e = t // 3, t % 3
        left = jnp.concatenate(
            [
                jnp.concatenate(
                    [xe[2 * o + a, e, 0:16].reshape(256, 128), xe[2 * o + a, e, 1:17].reshape(256, 128)], axis=1
                )
                for o in range(4)
            ],
            axis=0,
        )
        got = dot(left, flat1, 0, 0)
        for k in range(24):
            block = t * 24 + k
            g = block % 54 // 7
            s1[block // 54, g, block % 54 % 7] = got[64 + k * 8 : 64 + (k + 1) * 8].astype(BF)

    sum1.cores()

    def shift_delta(first, count):
        both = jnp.concatenate([d1e[first + k, 0, 0:16].reshape(256, 128) for k in range(count)], axis=1)
        got = dot(p3[...], both).astype(BF)
        for k in range(count):
            d1e[first + k, 1, 0:16] = got[:, k * 128 : (k + 1) * 128].reshape(16, 16, 128)

    def input_delta(pi, pj):
        @pl.loop(0, 4)
        def _(i):
            left, right = [], []
            for a, sa in taps_of[pi]:
                for e, se in taps_of[pj]:
                    left.append(d1e[i + sa, se, 0:16].reshape(256, 128))
                    left.append(d1e[i + sa, se, 1:17].reshape(256, 128))
                    t = a * 3 + e
                    right.append(wb[t * 256 : (t + 1) * 256])
            got = dot(jnp.concatenate(left, axis=1), jnp.concatenate(right, axis=0)).astype(BF)
            for q in range(16):
                un[2 * i + pi, pj * 16 : (pj + 1) * 16, q * 128 : (q + 1) * 128] = got[q * 16 : (q + 1) * 16]

    shift_delta(0, 2)
    shift_delta(2, 2)
    input_delta(0, 0)
    sum1.along_z()
    input_delta(0, 1)
    halo_d1.wait_recv()
    d1e[4, 0, 0:16] = jnp.where(top, jnp.zeros((16, 16, 128), BF), d1e[4, 0, 0:16])
    shift_delta(4, 1)
    input_delta(1, 0)
    input_delta(1, 1)

    @pl.loop(0, 8)
    def _(c):
        lanes = pl.ds(pl.multiple_of(c * 256, 256), 256)
        ig[:, lanes] = dot(p4[...], un[:, :, lanes].reshape(256, 256)).astype(BF)

    sum2.along_z()
    sum1.plane()
    sum2.gather_z()
    sum1.gather_plane()
    sum2.gather_plane()
    sum1.gather_z()
    sum2.finish()
    sum1.finish()
    for copy in sent + passed + [halo_in, halo_hid, halo_d2, halo_d1]:
        copy.wait_send()
    sum2.drain()
    sum1.drain()


def local(volume, weight_first, weight_second, cotangent):
    cells = 4 * lax.axis_size("space") * 4 * 256
    scales = (float(cells) ** -0.5, float(cells // 8) ** -0.5)
    vmem = pl.BlockSpec(memory_space=pltpu.VMEM)
    anywhere = pl.BlockSpec(memory_space=pl.ANY)
    far = pl.BlockSpec(memory_space=pltpu.HBM)
    shape = jax.ShapeDtypeStruct

    partial = pl.pallas_call(
        step_kernel,
        out_shape=(
            OUT((2, 8, 2048), BF),
            OUT((256, 2048), BF),
            OUT((NZ, 2 * NY, PIECE1, 128), BF),
            OUT((NY, 2, NZ, PIECE2, 128), BF),
        ),
        in_specs=[far] * 9,
        out_specs=(vmem,) * 4,
        scratch_shapes=[
            pltpu.VMEM((9, 3, 17, 16, 128), BF),
            pltpu.VMEM((32, 2048), BF),
            pltpu.VMEM((1728, 128), BF),
            pltpu.VMEM((2304, 128), BF),
            pltpu.VMEM((2304, 128), BF),
            pltpu.VMEM((3456, 256), BF),
            pltpu.VMEM((4, 256, 128), BF),
            pltpu.VMEM((256, 128), BF),
            pltpu.VMEM((4, 16, 16, 128), F32),
            pltpu.VMEM((128, 3456), BF),
            pltpu.VMEM((3, 64, 256), BF),
            pltpu.VMEM((3, 4, 64, 256), BF),
            pltpu.VMEM((5, 2, 17, 16, 128), BF),
            pltpu.VMEM((8, 32, 2048), BF),
            pltpu.SemaphoreType.DMA((2, 10)),
            pltpu.SemaphoreType.DMA((2, 4)),
        ]
        + LineReduction.scratch(PIECE1)
        + Reduction.scratch(PIECE2)
        + [
            pltpu.VMEM((256, 2048), BF),
            pltpu.VMEM((2, 8, 2048), BF),
            pltpu.VMEM((384, 256), BF),
            pltpu.VMEM((576, 256), BF),
            pltpu.VMEM((256, 64), BF),
            pltpu.VMEM((256, 256), BF),
            pltpu.VMEM((256, 256), BF),
            pltpu.SemaphoreType.DMA((9,)),
        ],
        compiler_params=pltpu.CompilerParams(
            collective_id=0, has_side_effects=True, vmem_limit_bytes=VLIM * 1024 * 1024
        ),
        name="step",
    )(
        *(
            pltpu.with_memory_space_constraint(x, pltpu.HBM)
            for x in (
                volume.reshape(256, 2048),
                weight_first,
                weight_second,
                cotangent.reshape(2, 8, 2048),
                *(jnp.asarray(m) for m in selections()),
            )
        )
    )

    def body(*refs):
        finish_kernel(scales, *refs)

    activations, input_gradient, first, second = pl.pallas_call(
        body,
        out_shape=(
            shape((2, 8, 2048), BF),
            shape((256, 2048), BF),
            shape((432, 128), F32),
            shape((864, 256), F32),
        ),
        in_specs=[vmem] * 4,
        out_specs=(anywhere, anywhere, vmem, vmem),
        scratch_shapes=[pltpu.SemaphoreType.DMA((2,))],
        compiler_params=pltpu.CompilerParams(vmem_limit_bytes=8 * 1024 * 1024),
        name="finish",
    )(*(pltpu.with_memory_space_constraint(x, pltpu.VMEM) for x in partial))
    return (
        activations.reshape(cotangent.shape),
        input_gradient.reshape(volume.shape),
        first,
        second,
    )


def solution(mesh):
    return jax.shard_map(
        local,
        mesh=mesh,
        in_specs=(
            P("dp", "space", None, None),
            P("dp", None),
            P("dp", None),
            P("dp", "space", None, None),
        ),
        out_specs=(
            P("dp", "space", None, None),
            P("dp", "space", None, None),
            P("dp", None),
            P("dp", None),
        ),
        check_vma=False,
    )
```

```python
import numpy as np

import jax
import jax.numpy as jnp
from jax import lax
from jax.experimental import pallas as pl
from jax.experimental.pallas import tpu as pltpu
from jax.sharding import PartitionSpec as P

NY, NZ = 4, 8
BF, F32 = jnp.bfloat16, jnp.float32
PIECE1, PIECE2 = 8, 32
GROUP1, GROUP2 = 56, 216
VLIM = 40
OUT = pltpu.VMEM
USED = 7
MESH = pl.DeviceIdType.MESH


def rank_of(p):
    return (p % 2) * 8 + p // 2


def selections():
    spread = np.zeros((48, 32), np.float32)
    shift = np.zeros((16, 16), np.float32)
    merge = np.zeros((32, 32), np.float32)
    for p in range(16):
        for e in range(3):
            if 2 * p - 1 + e >= 0:
                spread[e * 16 + rank_of(p), 2 * p - 1 + e] = 1
        if p < 15:
            shift[rank_of(p), rank_of(p + 1)] = 1
        for parity in range(2):
            merge[2 * p + parity, parity * 16 + rank_of(p)] = 1
    taps = np.zeros((3, 3, 8, 8, 16, 16), np.float32)
    moved = np.zeros((2, 2, 8, 8, 8, 8), np.float32)
    for p in range(8):
        for q in range(8):
            for e in range(3):
                for f in range(3):
                    j, l = 2 * p - 1 + e, 2 * q - 1 + f
                    if j >= 0 and l >= 0:
                        taps[e, f, q, p, l, rank_of(j)] = 1
            for a in range(2):
                for b in range(2):
                    if q + a < 8 and p + b < 8:
                        moved[a, b, q, p, q + a, p + b] = 1
    return tuple(
        m.astype(BF)
        for m in (
            np.kron(np.eye(8), spread),
            taps.reshape(576, 256),
            moved.reshape(256, 64),
            np.kron(np.eye(16), shift),
            np.kron(np.eye(8), merge),
        )
    )


def place():
    d, s = lax.axis_index("dp"), lax.axis_index("space")
    return d // 2, d % 2, s // (2 * NZ), (s // 2) % NZ, s % 2


def device(xl, core, y, z, xh):
    return {"dp": xl * 2 + core, "space": (y * NZ + z) * 2 + xh}


def remote(src, dst, sems, slot, target):
    copy = pltpu.make_async_remote_copy(
        src_ref=src,
        dst_ref=dst,
        send_sem=sems.at[0, slot],
        recv_sem=sems.at[1, slot],
        device_id=target,
        device_id_type=MESH,
    )
    copy.start()
    return copy


def dot(a, b, ca=1, cb=0):
    return lax.dot_general(a, b, (((ca,), (cb,)), ((), ())), preferred_element_type=F32)


def act_and_slope(v):
    t = jnp.exp(-jnp.abs(v))
    soft = jnp.maximum(v, 0.0) + jnp.log(1.0 + t)
    gate = jnp.where(v >= 0, 1.0, t) / (1.0 + t)
    return 0.2 * v + 0.8 * soft, 0.2 + 0.8 * gate


def far_first(n):
    return sorted(range(1, n), key=lambda k: -min(k, n - k))


COLUMNS = [(0, 1), (1, 0), (1, 1)]
CUT = 3


class Reduction:
    def __init__(self, s, bufs, sems, peers):
        self.s, self.sems, self.peers = s, sems, peers
        self.name(*bufs)
        self.copies = []
        self.slot = 0
        self.at = place()

    def name(self, r1, hy, r2, tx, r3x, ty, r3y, tot, r3, g):
        self.r1, self.hy, self.r2, self.tx, self.r3x, self.ty, self.r3y, self.tot = r1, hy, r2, tx, r3x, ty, r3y, tot
        self.r3, self.g = r3, g

    def send(self, src, dst, target):
        copy = remote(src, dst, self.sems, self.slot, target)
        self.slot += 1
        self.copies.append(copy)
        return copy

    def cores(self):
        xl, core, y, z, xh = self.at
        self.order = far_first(NY) + [0]
        self.first = {}
        for k in self.order:
            there = (y + k) % NY
            for h in range(2):
                self.first[k, h] = self.send(
                    self.s.at[h * 2 + 1 - core, there, :, pl.ds(0, USED)],
                    self.r1.at[k, h, :, pl.ds(0, USED)],
                    self.peers["core"],
                )

    def plane(self):
        xl, core, y, z, xh = self.at
        self.lines_x, self.lines_y = {}, {}
        for k in self.order:
            there = (y + k) % NY
            for h in range(2):
                self.first[k, h].wait_recv()
            for h in range(2):
                for v in range(2):
                    left = xl + h - 2 * xl * h
                    half = xh + v - 2 * xh * v
                    for i in range(USED):
                        mine = self.s[left * 2 + core, there, half, i].astype(F32)
                        self.hy[k, h, v, i] = (mine + self.r1[k, left, half, i].astype(F32)).astype(BF)
            if k:
                part = (k, slice(None), slice(None), pl.ds(CUT, USED - CUT))
                self.lines_y[k] = self.send(self.hy.at[part], self.r2.at[part], self.peers["plane", k, 0, 0])
        for h, v in COLUMNS:
            part = (slice(None), h, v, pl.ds(0, CUT))
            self.lines_x[h, v] = self.send(self.hy.at[part], self.r2.at[part], self.peers["plane", 0, h, v])

    def turn(self):
        self.second = []
        for copy in self.lines_x.values():
            copy.wait_recv()
        for k in self.order:
            for i in range(CUT):
                total = self.hy[k, 0, 0, i].astype(F32)
                for h, v in COLUMNS:
                    total += self.r2[k, h, v, i].astype(F32)
                self.tx[k, i] = total.astype(BF)
            if k:
                self.second.append(self.send(self.tx.at[k], self.r3x.at[k], self.peers["plane", k, 0, 0]))
        for copy in self.lines_y.values():
            copy.wait_recv()
        for h, v in COLUMNS + [(0, 0)]:
            for i in range(CUT, USED):
                total = self.hy[0, h, v, i].astype(F32)
                for k in range(1, NY):
                    total += self.r2[k, h, v, i].astype(F32)
                self.ty[h, v, i - CUT] = total.astype(BF)
            if h or v:
                self.second.append(self.send(self.ty.at[h, v], self.r3y.at[h, v], self.peers["plane", 0, h, v]))

    def along_z(self):
        xl, core, y, z, xh = self.at
        for copy in self.second:
            copy.wait_recv()
        for i in range(CUT):
            total = self.tx[0, i].astype(F32)
            for k in range(1, NY):
                total += self.r3x[k, i].astype(F32)
            self.tot[i] = total.astype(BF)
        for i in range(USED - CUT):
            total = self.ty[0, 0, i].astype(F32)
            for h, v in COLUMNS:
                total += self.r3y[h, v, i].astype(F32)
            self.tot[CUT + i] = total.astype(BF)
        self.tot[USED:] = jnp.zeros_like(self.tot[USED:])
        self.third = []
        for k in far_first(NZ):
            self.third.append(self.send(self.tot.at[(z + k) % NZ], self.r3.at[k - 1], self.peers["z", k]))

    def gather_z(self):
        xl, core, y, z, xh = self.at
        for copy in self.third:
            copy.wait_recv()
        total = self.tot[z].astype(F32)
        for j in range(NZ - 1):
            total += self.r3[j].astype(F32)
        self.g[y, xh, z] = total.astype(BF)
        self.fifth = {}
        for k in far_first(NZ):
            self.fifth[k] = self.send(self.g.at[y, xh, z], self.g.at[y, xh, z], self.peers["z", k])

    def gather_plane(self):
        xl, core, y, z, xh = self.at
        self.sixth = []
        for k in [0] + sorted(self.fifth, key=lambda k: min(k, NZ - k)):
            if k:
                self.fifth[k].wait_recv()
            part = self.g.at[y, xh, (z + NZ - k) % NZ]
            for j in far_first(NY) + [0]:
                for v in (1, 0):
                    if (j, v) != (0, 0):
                        self.sixth.append(self.send(part, part, self.peers["plane", j, 0, v]))

    def finish(self):
        for copy in self.sixth:
            copy.wait_recv()

    def drain(self):
        for copy in self.copies:
            copy.wait_send()

    @staticmethod
    def scratch(piece):
        blocks = (NY, 2, 2, NZ, piece, 128)
        return [
            pltpu.VMEM((4, NY, 2, NZ, piece, 128), BF),
            pltpu.VMEM(blocks, BF),
            pltpu.VMEM(blocks, BF),
            pltpu.VMEM(blocks, BF),
            pltpu.VMEM((NY, CUT, piece, 128), BF),
            pltpu.VMEM((NY, CUT, piece, 128), BF),
            pltpu.VMEM((2, 2, USED - CUT, piece, 128), BF),
            pltpu.VMEM((2, 2, USED - CUT, piece, 128), BF),
            pltpu.VMEM((NZ, piece, 128), BF),
            pltpu.VMEM((NZ - 1, piece, 128), BF),
            pltpu.SemaphoreType.DMA((2, 2 * NY + 2 * (NY + 2) + 2 * (NZ - 1) + NZ * (2 * NY - 1))),
        ]


class LineReduction(Reduction):
    def name(self, r1, hy, r2, hz, r3, g):
        self.r1, self.hy, self.r2, self.hz, self.r3, self.g = r1, hy, r2, hz, r3, g

    def cores(self):
        xl, core, y, z, xh = self.at
        self.first = []
        for h in range(2):
            self.first.append(
                self.send(
                    self.s.at[h * 2 + 1 - core, :, pl.ds(0, USED)], self.r1.at[h, :, pl.ds(0, USED)], self.peers["core"]
                )
            )

    def along_z(self):
        xl, core, y, z, xh = self.at
        for copy in self.first:
            copy.wait_recv()
        self.second = []
        for k in far_first(NZ) + [0]:
            there = (z + k) % NZ
            for h in range(2):
                for i in range(USED):
                    mine = self.s[h * 2 + core, there, i].astype(F32)
                    self.hy[k, h, i] = (mine + self.r1[h, there, i].astype(F32)).astype(BF)
            if k:
                self.second.append(
                    self.send(
                        self.hy.at[k, :, pl.ds(0, USED)], self.r2.at[k - 1, :, pl.ds(0, USED)], self.peers["z", k]
                    )
                )

    def plane(self):
        xl, core, y, z, xh = self.at
        for copy in self.second:
            copy.wait_recv()
        for h in range(2):
            for i in range(USED):
                total = self.hy[0, h, i].astype(F32)
                for j in range(NZ - 1):
                    total += self.r2[j, h, i].astype(F32)
                self.hz[h, i] = total.astype(BF)
            self.hz[h, USED:] = jnp.zeros_like(self.hz[h, USED:])
        self.third = []
        for k in far_first(NY) + [0]:
            for h in range(2):
                for v in range(2):
                    if (k, h, v) != (0, 0, 0):
                        left = xl + h - 2 * xl * h
                        group = (y + k) % NY * 2 + xh + v - 2 * xh * v
                        self.third.append(
                            self.send(self.hz.at[left, group], self.r3.at[k, h, v], self.peers["plane", k, h, v])
                        )

    def gather_plane(self):
        xl, core, y, z, xh = self.at
        for copy in self.third:
            copy.wait_recv()
        mine = y * 2 + xh
        total = self.hz[xl, mine].astype(F32)
        for k in range(NY):
            for h in range(2):
                for v in range(2):
                    if (k, h, v) != (0, 0, 0):
                        total += self.r3[k, h, v].astype(F32)
        self.g[z, mine] = total.astype(BF)
        self.fifth = {}
        for k in far_first(NY) + [0]:
            for v in (1, 0):
                if (k, v) != (0, 0):
                    self.fifth[k, v] = self.send(self.g.at[z, mine], self.g.at[z, mine], self.peers["plane", k, 0, v])

    def gather_z(self):
        xl, core, y, z, xh = self.at
        self.sixth = []
        for k, v in [(0, 0)] + sorted(self.fifth, key=lambda kv: min(kv[0], NY - kv[0]) + 2 * kv[1]):
            if (k, v) != (0, 0):
                self.fifth[k, v].wait_recv()
            part = self.g.at[z, (y + NY - k) % NY * 2 + xh + v - 2 * xh * v]
            for j in far_first(NZ):
                self.sixth.append(self.send(part, part, self.peers["z", j]))

    @staticmethod
    def scratch(piece):
        return [
            pltpu.VMEM((4, NZ, 2 * NY, piece, 128), BF),
            pltpu.VMEM((2, NZ, 2 * NY, piece, 128), BF),
            pltpu.VMEM((NZ, 2, 2 * NY, piece, 128), BF),
            pltpu.VMEM((NZ - 1, 2, 2 * NY, piece, 128), BF),
            pltpu.VMEM((2, 2 * NY, piece, 128), BF),
            pltpu.VMEM((NY, 2, 2, piece, 128), BF),
            pltpu.SemaphoreType.DMA((2, 2 + (NZ - 1) + (4 * NY - 1) + (2 * NY - 1) + 2 * NY * (NZ - 1))),
        ]


def pieces(lo, hi, group, piece):
    while lo < hi:
        where = lo % group
        count = min(hi - lo, group - where, piece - where % piece)
        yield lo, count, lo // group, where // piece, where % piece
        lo += count


def finish_kernel(scales, actv, ig, g1, g2, actv_out, ig_out, g1out, g2out, sems):
    copies = [pltpu.make_async_copy(ig, ig_out, sems.at[0]), pltpu.make_async_copy(actv, actv_out, sems.at[1])]
    for copy in copies:
        copy.start()
    for row, count, g, k, at_row in pieces(0, 1728, GROUP2, PIECE2):
        got = g2[g // 2, g % 2, k, at_row : at_row + count].astype(F32) * scales[1]
        half = row // 864
        g2out[row % 864 : row % 864 + count, half * 128 : (half + 1) * 128] = got
    for row, count, g, k, at_row in pieces(0, 432, GROUP1, PIECE1):
        g1out[row : row + count] = g1[g, k].astype(F32) * scales[0]
    for copy in copies:
        copy.wait()


def step_kernel(vol_in, w1, w2, cot_in, p0_in, p1_in, p2_in, p3_in, p4_in, actv, ig, g1, g2, *scratch):
    vol, cot, p0, p1, p2, p3, p4, lsem = scratch[35:]
    loads = []
    for k, (src, dst) in enumerate(
        ((vol_in, vol), (p0_in, p0), (p1_in, p1), (cot_in, cot), (p2_in, p2), (p3_in, p3), (p4_in, p4))
    ):
        loads.append(pltpu.make_async_copy(src, dst, lsem.at[k]))
        loads[-1].start()
    xe, xhalo, partial, w1g, w1p, wb, w2g, hid, hhalo, slope, l2, d2, d2e, d1e, un = scratch[:15]
    wsem, hsem = scratch[15:17]
    s1, *bufs1, sems1 = scratch[17:24]
    s2, *bufs2, sems2 = scratch[24:35]
    bufs1.append(g1)
    bufs2.append(g2)
    at = xl, core, y, z, xh = place()
    s, d = lax.axis_index("space"), lax.axis_index("dp")
    n = 2 * NY * NZ
    bottom, top = s == 0, s == n - 1
    upper = {"space": (s + 1) % n}
    lower = {"space": (s + n - 1) % n}
    peers = {"core": device(xl, 1 - core, y, z, xh)}
    for k in range(NY):
        for h in range(2):
            for v in range(2):
                if (k, h, v) != (0, 0, 0):
                    there = xl + h - 2 * xl * h, core, (y + k) % NY, z, xh + v - 2 * xh * v
                    peers["plane", k, h, v] = device(*there)
    for k in range(1, NZ):
        peers["z", k] = device(xl, core, y, (z + k) % NZ, xh)
    peers["upper"], peers["lower"] = upper, lower

    held = []
    for k, (src, dst, size) in enumerate(((w1, w1g, 432), (w2, w2g, 864))):
        at_rows = pl.ds(pl.multiple_of(d * size, 16), size)
        held.append(pltpu.make_async_copy(src, dst.at[at_rows], lsem.at[7 + k]))
        held[-1].start()

    barrier = pltpu.get_barrier_semaphore()
    for peer in peers.values():
        pl.semaphore_signal(barrier, inc=1, device_id=peer, device_id_type=MESH)
    pl.semaphore_wait(barrier, len(peers))

    def rows(q, size, lo, hi):
        return pl.ds(pl.multiple_of(q * size + lo, 16), hi - lo)

    def weight(source, whole, size, cuts, base):
        chunks, slot = [], base
        middle = len(cuts) // 2
        for k in range(middle):
            chunk = []
            for j, peer in ((k, peers["plane", 0, 1, 0]), (middle + k, peers["plane", 0, 1, 1])):
                lo, hi = cuts[j], cuts[j + 1]
                part = source.at[pl.ds(lo, hi - lo)]
                chunk.append((lo, hi, remote(part, whole.at[rows(d, size, lo, hi)], wsem, slot, peer), slot + 1))
                slot += 2
            chunks.append(chunk)
        to_core = remote(source, whole.at[rows(d, size, 0, size)], wsem, slot, peers["core"])
        sent.extend([c[2] for chunk in chunks for c in chunk] + [to_core])
        return chunks, to_core

    sent, passed = [], []
    theirs = (1 - xl) * 2 + core
    chunks1, to_core1 = weight(w1, w1g, 432, (0, 224, 432), 0)
    chunks2, to_core2 = weight(w2, w2g, 864, (0, 224, 432, 656, 864), 5)

    def pass_on(whole, size, chunk):
        for lo, hi, copy, slot in chunk:
            copy.wait_recv()
            part = whole.at[rows(theirs, size, lo, hi)]
            passed.append(remote(part, part, wsem, slot, peers["core"]))

    xe[:, :, 0] = jnp.zeros((9, 3, 16, 128), BF)
    for copy in loads + held:
        copy.wait()

    @pl.loop(0, 8)
    def _(c):
        got = dot(p0[...], vol[:, pl.ds(pl.multiple_of(c * 256, 256), 256)]).astype(BF)
        for i in range(8):
            for e in range(3):
                for u in range(2):
                    xe[i + 1, e, 2 * c + 1 + u] = got[(i * 3 + e) * 16 : (i * 3 + e + 1) * 16, u * 128 : (u + 1) * 128]

    pass_on(w1g, 432, chunks1[0])
    for copy in [to_core1] + passed:
        copy.wait_recv()
    for t in range(9):
        w1p[t * 256 : t * 256 + 64] = jnp.zeros((64, 128), BF)
        w1p[t * 256 + 64 : t * 256 + 256] = w1g[t * 192 : (t + 1) * 192]

    def pairs(plane, taps):
        tiles = []
        for a in taps:
            for e in range(3):
                tiles.append(xe[plane + a, e, 0:16].reshape(256, 128))
                tiles.append(xe[plane + a, e, 1:17].reshape(256, 128))
        return jnp.concatenate(tiles, axis=1)

    def finish_first(o, linear):
        value, gate = act_and_slope(linear)
        hid[o] = value.astype(BF)
        slope[o] = gate.reshape(16, 16, 128)

    partial[...] = dot(pairs(8, (0,)), w1p[0:768]).astype(BF)
    halo_in = remote(partial, xhalo, hsem, 0, upper)
    finish_first(3, dot(pairs(6, range(3)), w1p[...]))
    halo_hid = remote(hid.at[3], hhalo, hsem, 1, upper)
    pass_on(w2g, 864, chunks2[0])

    @pl.loop(1, 3)
    def _(o):
        finish_first(o, dot(pairs(2 * o, range(3)), w1p[...]))

    pass_on(w2g, 864, chunks2[1])
    local_first = dot(pairs(0, (1, 2)), w1p[768:])
    halo_in.wait_recv()
    finish_first(0, local_first + jnp.where(bottom, 0.0, xhalo[...].astype(F32)))

    def place_taps(got, plane):
        for o in range(2):
            a = plane - 2 * o
            if 0 <= a < 3:
                for k in range(9):
                    l2[o * 64 : (o + 1) * 64, (a * 9 + k) * 128 : (a * 9 + k + 1) * 128] = got[k * 64 : (k + 1) * 64]

    for pair in range(2):
        both = jnp.concatenate([hid[2 * pair], hid[2 * pair + 1]], axis=1)
        got = dot(p1[...], both).astype(BF)
        place_taps(got[:, :128], 2 * pair + 1)
        place_taps(got[:, 128:], 2 * pair + 2)
    for t in range(9):
        block = w1p[t * 256 : (t + 1) * 256]
        wb[t * 256 : t * 256 + 128] = block[128:].T
        wb[t * 256 + 128 : (t + 1) * 256] = block[:128].T
    halo_hid.wait_recv()
    rim = jnp.where(bottom, jnp.zeros_like(hhalo), hhalo[...])
    place_taps(dot(p1[...], rim).astype(BF), 0)
    for copy in [to_core2] + passed[2:]:
        copy.wait_recv()

    linear = dot(l2[...], w2g[...])
    value, gate = act_and_slope(linear)
    arriving = jnp.concatenate(
        [cot[o, :, q * 256 : (q + 1) * 256].astype(F32) for o in range(2) for q in range(8)], axis=0
    )
    delta = (arriving * gate).astype(BF)
    d2[0] = delta[:64]
    halo_d2 = remote(d2.at[0], d2.at[2], hsem, 2, lower)
    d2[1] = delta[64:]
    for o in range(2):
        for q in range(8):
            at_row = (o * 8 + q) * 8
            actv[o, :, q * 256 : (q + 1) * 256] = value[at_row : at_row + 8].astype(BF)

    for t in range(27):
        got = dot(l2[:, t * 128 : (t + 1) * 128], delta, 0, 0)
        for q in range(4):
            lo, hi = max(t * 128, q * 864), min(t * 128 + 128, q * 864 + 864)
            for row, count, g, k, at_row in pieces(lo - q * 864, hi - q * 864, GROUP2, PIECE2):
                row += q * 864 - t * 128
                for half in range(2):
                    block = got[row : row + count, half * 128 : (half + 1) * 128].astype(BF)
                    h = half * NY + g
                    s2[q, h // 2, h % 2, k, at_row : at_row + count] = block
    sum2 = Reduction(s2, bufs2, sems2, peers)
    sum1 = LineReduction(s1, bufs1, sems1, peers)
    sum2.cores()

    def spread_delta(o):
        got = dot(p2[...], d2[o]).astype(BF)
        for v in range(4):
            d2e[o, v] = got[v * 64 : (v + 1) * 64]

    taps_of = (((1, 0),), ((2, 0), (0, 1)))

    def hidden_delta(pi):
        for pq in range(2):
            halves = []
            for pj in range(2):
                left, right = [], []
                for a, sa in taps_of[pi]:
                    for e, se in taps_of[pj]:
                        for f, sf in taps_of[pq]:
                            left.append(d2e[sa : sa + 2, sf * 2 + se].reshape(128, 256))
                            t = a * 9 + e * 3 + f
                            right.append(w2g[t * 128 : (t + 1) * 128])
                got = dot(jnp.concatenate(left, axis=1), jnp.concatenate(right, axis=1), 1, 1)
                halves.append(got.reshape(2, 8, 8, 128))
            both = jnp.concatenate(halves, axis=2)
            for i in range(2):
                for q in range(8):
                    d1e[2 * i + pi, 0, 2 * q + pq] = (both[i, q] * slope[2 * i + pi, 2 * q + pq]).astype(BF)

    spread_delta(0)
    spread_delta(1)
    d1e[:, :, 16] = jnp.zeros((5, 2, 16, 128), BF)
    hidden_delta(0)
    halo_d1 = remote(d1e.at[0, 0, pl.ds(0, 16)], d1e.at[4, 0, pl.ds(0, 16)], hsem, 3, lower)
    sum2.plane()
    halo_d2.wait_recv()
    d2[2] = jnp.where(top, jnp.zeros((64, 256), BF), d2[2])
    spread_delta(2)
    hidden_delta(1)

    def first_gradient(start, stop, shift):
        right = jnp.concatenate([d1e[o + shift, 0, 0:16].reshape(256, 128) for o in range(4)], axis=0)

        @pl.loop(start, stop)
        def _(t):
            a, e = t // 3, t % 3
            left = []
            for o in range(4):
                plane = 2 * (o + shift) + a
                left.append(
                    jnp.concatenate(
                        [xe[plane, e, 0:16].reshape(256, 128), xe[plane, e, 1:17].reshape(256, 128)], axis=1
                    )
                )
            got = dot(jnp.concatenate(left, axis=0), right, 0, 0)
            for k in range(24):
                block = t * 24 + k
                g = block % 54 // 7
                s1[block // 54, g, block % 54 % 7] = got[64 + k * 8 : 64 + (k + 1) * 8].astype(BF)

    first_gradient(3, 9, 0)
    halo_d1.wait_recv()
    d1e[4, 0, 0:16] = jnp.where(top, jnp.zeros((16, 16, 128), BF), d1e[4, 0, 0:16])
    first_gradient(0, 3, 1)
    sum1.cores()

    def shift_delta(first, count):
        both = jnp.concatenate([d1e[first + k, 0, 0:16].reshape(256, 128) for k in range(count)], axis=1)
        got = dot(p3[...], both).astype(BF)
        for k in range(count):
            d1e[first + k, 1, 0:16] = got[:, k * 128 : (k + 1) * 128].reshape(16, 16, 128)

    def input_delta(pi, pj):
        @pl.loop(0, 4)
        def _(i):
            left, right = [], []
            for a, sa in taps_of[pi]:
                for e, se in taps_of[pj]:
                    left.append(d1e[i + sa, se, 0:16].reshape(256, 128))
                    left.append(d1e[i + sa, se, 1:17].reshape(256, 128))
                    t = a * 3 + e
                    right.append(wb[t * 256 : (t + 1) * 256])
            got = dot(jnp.concatenate(left, axis=1), jnp.concatenate(right, axis=0)).astype(BF)
            for q in range(16):
                un[2 * i + pi, pj * 16 : (pj + 1) * 16, q * 128 : (q + 1) * 128] = got[q * 16 : (q + 1) * 16]

    shift_delta(0, 2)
    shift_delta(2, 2)
    input_delta(0, 0)
    sum1.along_z()
    sum2.turn()
    input_delta(0, 1)
    shift_delta(4, 1)
    input_delta(1, 0)
    input_delta(1, 1)

    @pl.loop(0, 8)
    def _(c):
        lanes = pl.ds(pl.multiple_of(c * 256, 256), 256)
        ig[:, lanes] = dot(p4[...], un[:, :, lanes].reshape(256, 256)).astype(BF)

    sum2.along_z()
    sum1.plane()
    sum2.gather_z()
    sum1.gather_plane()
    sum2.gather_plane()
    sum1.gather_z()
    sum2.finish()
    sum1.finish()
    for copy in sent + passed + [halo_in, halo_hid, halo_d2, halo_d1]:
        copy.wait_send()
    sum2.drain()
    sum1.drain()


def local(volume, weight_first, weight_second, cotangent):
    cells = 4 * lax.axis_size("space") * 4 * 256
    scales = (float(cells) ** -0.5, float(cells // 8) ** -0.5)
    vmem = pl.BlockSpec(memory_space=pltpu.VMEM)
    anywhere = pl.BlockSpec(memory_space=pl.ANY)
    far = pl.BlockSpec(memory_space=pltpu.HBM)
    shape = jax.ShapeDtypeStruct

    partial = pl.pallas_call(
        step_kernel,
        out_shape=(
            OUT((2, 8, 2048), BF),
            OUT((256, 2048), BF),
            OUT((NZ, 2 * NY, PIECE1, 128), BF),
            OUT((NY, 2, NZ, PIECE2, 128), BF),
        ),
        in_specs=[far] * 9,
        out_specs=(vmem,) * 4,
        scratch_shapes=[
            pltpu.VMEM((9, 3, 17, 16, 128), BF),
            pltpu.VMEM((256, 128), BF),
            pltpu.VMEM((256, 128), BF),
            pltpu.VMEM((1728, 128), BF),
            pltpu.VMEM((2304, 128), BF),
            pltpu.VMEM((2304, 128), BF),
            pltpu.VMEM((3456, 256), BF),
            pltpu.VMEM((4, 256, 128), BF),
            pltpu.VMEM((256, 128), BF),
            pltpu.VMEM((4, 16, 16, 128), F32),
            pltpu.VMEM((128, 3456), BF),
            pltpu.VMEM((3, 64, 256), BF),
            pltpu.VMEM((3, 4, 64, 256), BF),
            pltpu.VMEM((5, 2, 17, 16, 128), BF),
            pltpu.VMEM((8, 32, 2048), BF),
            pltpu.SemaphoreType.DMA((2, 14)),
            pltpu.SemaphoreType.DMA((2, 4)),
        ]
        + LineReduction.scratch(PIECE1)
        + Reduction.scratch(PIECE2)
        + [
            pltpu.VMEM((256, 2048), BF),
            pltpu.VMEM((2, 8, 2048), BF),
            pltpu.VMEM((384, 256), BF),
            pltpu.VMEM((576, 256), BF),
            pltpu.VMEM((256, 64), BF),
            pltpu.VMEM((256, 256), BF),
            pltpu.VMEM((256, 256), BF),
            pltpu.SemaphoreType.DMA((9,)),
        ],
        compiler_params=pltpu.CompilerParams(
            collective_id=0, has_side_effects=True, vmem_limit_bytes=VLIM * 1024 * 1024
        ),
        name="step",
    )(
        *(
            pltpu.with_memory_space_constraint(x, pltpu.HBM)
            for x in (
                volume.reshape(256, 2048),
                weight_first,
                weight_second,
                cotangent.reshape(2, 8, 2048),
                *(jnp.asarray(m) for m in selections()),
            )
        )
    )

    def body(*refs):
        finish_kernel(scales, *refs)

    activations, input_gradient, first, second = pl.pallas_call(
        body,
        out_shape=(
            shape((2, 8, 2048), BF),
            shape((256, 2048), BF),
            shape((432, 128), F32),
            shape((864, 256), F32),
        ),
        in_specs=[vmem] * 4,
        out_specs=(anywhere, anywhere, vmem, vmem),
        scratch_shapes=[pltpu.SemaphoreType.DMA((2,))],
        compiler_params=pltpu.CompilerParams(vmem_limit_bytes=8 * 1024 * 1024),
        name="finish",
    )(*(pltpu.with_memory_space_constraint(x, pltpu.VMEM) for x in partial))
    return (
        activations.reshape(cotangent.shape),
        input_gradient.reshape(volume.shape),
        first,
        second,
    )


def solution(mesh):
    return jax.shard_map(
        local,
        mesh=mesh,
        in_specs=(
            P("dp", "space", None, None),
            P("dp", None),
            P("dp", None),
            P("dp", "space", None, None),
        ),
        out_specs=(
            P("dp", "space", None, None),
            P("dp", "space", None, None),
            P("dp", None),
            P("dp", None),
        ),
        check_vma=False,
    )
```

```python
import numpy as np

import jax
import jax.numpy as jnp
from jax import lax
from jax.experimental import pallas as pl
from jax.experimental.pallas import tpu as pltpu
from jax.sharding import PartitionSpec as P

NY, NZ = 4, 8
BF, F32 = jnp.bfloat16, jnp.float32
PIECE1, PIECE2 = 8, 32
GROUP1, GROUP2 = 56, 216
VLIM = 40
OUT = pltpu.VMEM
USED = 7
MESH = pl.DeviceIdType.MESH


def rank_of(p):
    return (p % 2) * 8 + p // 2


def selections():
    spread = np.zeros((48, 32), np.float32)
    shift = np.zeros((16, 16), np.float32)
    merge = np.zeros((32, 32), np.float32)
    for p in range(16):
        for e in range(3):
            if 2 * p - 1 + e >= 0:
                spread[e * 16 + rank_of(p), 2 * p - 1 + e] = 1
        if p < 15:
            shift[rank_of(p), rank_of(p + 1)] = 1
        for parity in range(2):
            merge[2 * p + parity, parity * 16 + rank_of(p)] = 1
    taps = np.zeros((3, 3, 8, 8, 16, 16), np.float32)
    moved = np.zeros((2, 2, 8, 8, 8, 8), np.float32)
    for p in range(8):
        for q in range(8):
            for e in range(3):
                for f in range(3):
                    j, l = 2 * p - 1 + e, 2 * q - 1 + f
                    if j >= 0 and l >= 0:
                        taps[e, f, q, p, l, rank_of(j)] = 1
            for a in range(2):
                for b in range(2):
                    if q + a < 8 and p + b < 8:
                        moved[a, b, q, p, q + a, p + b] = 1
    return tuple(
        m.astype(BF)
        for m in (
            np.kron(np.eye(8), spread),
            taps.reshape(576, 256),
            moved.reshape(256, 64),
            np.kron(np.eye(16), shift),
            np.kron(np.eye(8), merge),
        )
    )


def place():
    d, s = lax.axis_index("dp"), lax.axis_index("space")
    return d // 2, d % 2, s // (2 * NZ), (s // 2) % NZ, s % 2


def device(xl, core, y, z, xh):
    return {"dp": xl * 2 + core, "space": (y * NZ + z) * 2 + xh}


def remote(src, dst, sems, slot, target):
    copy = pltpu.make_async_remote_copy(
        src_ref=src,
        dst_ref=dst,
        send_sem=sems.at[0, slot],
        recv_sem=sems.at[1, slot],
        device_id=target,
        device_id_type=MESH,
    )
    copy.start()
    return copy


def dot(a, b, ca=1, cb=0):
    return lax.dot_general(a, b, (((ca,), (cb,)), ((), ())), preferred_element_type=F32)


def act_and_slope(v):
    t = jnp.exp(-jnp.abs(v))
    soft = jnp.maximum(v, 0.0) + jnp.log(1.0 + t)
    gate = jnp.where(v >= 0, 1.0, t) / (1.0 + t)
    return 0.2 * v + 0.8 * soft, 0.2 + 0.8 * gate


def far_first(n):
    return sorted(range(1, n), key=lambda k: -min(k, n - k))


COLUMNS = [(0, 1), (1, 0), (1, 1)]
CUT = 3


class Reduction:
    def __init__(self, s, bufs, sems, peers):
        self.s, self.sems, self.peers = s, sems, peers
        self.name(*bufs)
        self.copies = []
        self.slot = 0
        self.at = place()

    def name(self, r1, hy, r2, tx, r3x, ty, r3y, tot, r3, g):
        self.r1, self.hy, self.r2, self.tx, self.r3x, self.ty, self.r3y, self.tot = r1, hy, r2, tx, r3x, ty, r3y, tot
        self.r3, self.g = r3, g

    def send(self, src, dst, target):
        copy = remote(src, dst, self.sems, self.slot, target)
        self.slot += 1
        self.copies.append(copy)
        return copy

    def cores(self):
        xl, core, y, z, xh = self.at
        self.order = far_first(NY) + [0]
        self.first = {}
        for k in self.order:
            there = (y + k) % NY
            for h in range(2):
                self.first[k, h] = self.send(
                    self.s.at[h * 2 + 1 - core, there, :, pl.ds(0, USED)],
                    self.r1.at[k, h, :, pl.ds(0, USED)],
                    self.peers["core"],
                )

    def plane(self):
        xl, core, y, z, xh = self.at
        self.lines_x, self.lines_y = {}, {}
        for k in self.order:
            there = (y + k) % NY
            for h in range(2):
                self.first[k, h].wait_recv()
            for h in range(2):
                for v in range(2):
                    left = xl + h - 2 * xl * h
                    half = xh + v - 2 * xh * v
                    for i in range(USED):
                        mine = self.s[left * 2 + core, there, half, i].astype(F32)
                        self.hy[k, h, v, i] = (mine + self.r1[k, left, half, i].astype(F32)).astype(BF)
            if k:
                part = (k, slice(None), slice(None), pl.ds(CUT, USED - CUT))
                self.lines_y[k] = self.send(self.hy.at[part], self.r2.at[part], self.peers["plane", k, 0, 0])
        for h, v in COLUMNS:
            part = (slice(None), h, v, pl.ds(0, CUT))
            self.lines_x[h, v] = self.send(self.hy.at[part], self.r2.at[part], self.peers["plane", 0, h, v])

    def turn(self):
        self.second = []
        for copy in self.lines_x.values():
            copy.wait_recv()
        for k in self.order:
            for i in range(CUT):
                total = self.hy[k, 0, 0, i].astype(F32)
                for h, v in COLUMNS:
                    total += self.r2[k, h, v, i].astype(F32)
                self.tx[k, i] = total.astype(BF)
            if k:
                self.second.append(self.send(self.tx.at[k], self.r3x.at[k], self.peers["plane", k, 0, 0]))
        for copy in self.lines_y.values():
            copy.wait_recv()
        for h, v in COLUMNS + [(0, 0)]:
            for i in range(CUT, USED):
                total = self.hy[0, h, v, i].astype(F32)
                for k in range(1, NY):
                    total += self.r2[k, h, v, i].astype(F32)
                self.ty[h, v, i - CUT] = total.astype(BF)
            if h or v:
                self.second.append(self.send(self.ty.at[h, v], self.r3y.at[h, v], self.peers["plane", 0, h, v]))

    def along_z(self):
        xl, core, y, z, xh = self.at
        for copy in self.second:
            copy.wait_recv()
        for i in range(CUT):
            total = self.tx[0, i].astype(F32)
            for k in range(1, NY):
                total += self.r3x[k, i].astype(F32)
            self.tot[i] = total.astype(BF)
        for i in range(USED - CUT):
            total = self.ty[0, 0, i].astype(F32)
            for h, v in COLUMNS:
                total += self.r3y[h, v, i].astype(F32)
            self.tot[CUT + i] = total.astype(BF)
        self.tot[USED:] = jnp.zeros_like(self.tot[USED:])
        self.third = []
        for k in far_first(NZ):
            self.third.append(self.send(self.tot.at[(z + k) % NZ], self.r3.at[k - 1], self.peers["z", k]))

    def gather_z(self):
        xl, core, y, z, xh = self.at
        for copy in self.third:
            copy.wait_recv()
        total = self.tot[z].astype(F32)
        for j in range(NZ - 1):
            total += self.r3[j].astype(F32)
        self.g[y, xh, z] = total.astype(BF)
        self.fifth = {}
        for k in far_first(NZ):
            self.fifth[k] = self.send(self.g.at[y, xh, z], self.g.at[y, xh, z], self.peers["z", k])

    def gather_plane(self):
        xl, core, y, z, xh = self.at
        self.sixth = []
        for k in [0] + sorted(self.fifth, key=lambda k: min(k, NZ - k)):
            if k:
                self.fifth[k].wait_recv()
            part = self.g.at[y, xh, (z + NZ - k) % NZ]
            for j in far_first(NY) + [0]:
                for v in (1, 0):
                    if (j, v) != (0, 0):
                        self.sixth.append(self.send(part, part, self.peers["plane", j, 0, v]))

    def finish(self):
        for copy in self.sixth:
            copy.wait_recv()

    def drain(self):
        for copy in self.copies:
            copy.wait_send()

    @staticmethod
    def scratch(piece):
        blocks = (NY, 2, 2, NZ, piece, 128)
        return [
            pltpu.VMEM((4, NY, 2, NZ, piece, 128), BF),
            pltpu.VMEM(blocks, BF),
            pltpu.VMEM(blocks, BF),
            pltpu.VMEM(blocks, BF),
            pltpu.VMEM((NY, CUT, piece, 128), BF),
            pltpu.VMEM((NY, CUT, piece, 128), BF),
            pltpu.VMEM((2, 2, USED - CUT, piece, 128), BF),
            pltpu.VMEM((2, 2, USED - CUT, piece, 128), BF),
            pltpu.VMEM((NZ, piece, 128), BF),
            pltpu.VMEM((NZ - 1, piece, 128), BF),
            pltpu.SemaphoreType.DMA((2, 2 * NY + 2 * (NY + 2) + 2 * (NZ - 1) + NZ * (2 * NY - 1))),
        ]


class LineReduction(Reduction):
    def name(self, r1, hy, r2, hz, r3, g):
        self.r1, self.hy, self.r2, self.hz, self.r3, self.g = r1, hy, r2, hz, r3, g

    def cores(self):
        xl, core, y, z, xh = self.at
        self.first = []
        for h in range(2):
            self.first.append(
                self.send(
                    self.s.at[h * 2 + 1 - core, :, pl.ds(0, USED)], self.r1.at[h, :, pl.ds(0, USED)], self.peers["core"]
                )
            )

    def along_z(self):
        xl, core, y, z, xh = self.at
        for copy in self.first:
            copy.wait_recv()
        self.second = []
        for k in far_first(NZ) + [0]:
            there = (z + k) % NZ
            for h in range(2):
                for i in range(USED):
                    mine = self.s[h * 2 + core, there, i].astype(F32)
                    self.hy[k, h, i] = (mine + self.r1[h, there, i].astype(F32)).astype(BF)
            if k:
                self.second.append(
                    self.send(
                        self.hy.at[k, :, pl.ds(0, USED)], self.r2.at[k - 1, :, pl.ds(0, USED)], self.peers["z", k]
                    )
                )

    def plane(self):
        xl, core, y, z, xh = self.at
        for copy in self.second:
            copy.wait_recv()
        for h in range(2):
            for i in range(USED):
                total = self.hy[0, h, i].astype(F32)
                for j in range(NZ - 1):
                    total += self.r2[j, h, i].astype(F32)
                self.hz[h, i] = total.astype(BF)
            self.hz[h, USED:] = jnp.zeros_like(self.hz[h, USED:])
        self.third = []
        for k in far_first(NY) + [0]:
            for h in range(2):
                for v in range(2):
                    if (k, h, v) != (0, 0, 0):
                        left = xl + h - 2 * xl * h
                        group = (y + k) % NY * 2 + xh + v - 2 * xh * v
                        self.third.append(
                            self.send(self.hz.at[left, group], self.r3.at[k, h, v], self.peers["plane", k, h, v])
                        )

    def gather_plane(self):
        xl, core, y, z, xh = self.at
        for copy in self.third:
            copy.wait_recv()
        mine = y * 2 + xh
        total = self.hz[xl, mine].astype(F32)
        for k in range(NY):
            for h in range(2):
                for v in range(2):
                    if (k, h, v) != (0, 0, 0):
                        total += self.r3[k, h, v].astype(F32)
        self.g[z, mine] = total.astype(BF)
        self.fifth = {}
        for k in far_first(NY) + [0]:
            for v in (1, 0):
                if (k, v) != (0, 0):
                    self.fifth[k, v] = self.send(self.g.at[z, mine], self.g.at[z, mine], self.peers["plane", k, 0, v])

    def gather_z(self):
        xl, core, y, z, xh = self.at
        self.sixth = []
        for k, v in [(0, 0)] + sorted(self.fifth, key=lambda kv: min(kv[0], NY - kv[0]) + 2 * kv[1]):
            if (k, v) != (0, 0):
                self.fifth[k, v].wait_recv()
            part = self.g.at[z, (y + NY - k) % NY * 2 + xh + v - 2 * xh * v]
            for j in far_first(NZ):
                self.sixth.append(self.send(part, part, self.peers["z", j]))

    @staticmethod
    def scratch(piece):
        return [
            pltpu.VMEM((4, NZ, 2 * NY, piece, 128), BF),
            pltpu.VMEM((2, NZ, 2 * NY, piece, 128), BF),
            pltpu.VMEM((NZ, 2, 2 * NY, piece, 128), BF),
            pltpu.VMEM((NZ - 1, 2, 2 * NY, piece, 128), BF),
            pltpu.VMEM((2, 2 * NY, piece, 128), BF),
            pltpu.VMEM((NY, 2, 2, piece, 128), BF),
            pltpu.SemaphoreType.DMA((2, 2 + (NZ - 1) + (4 * NY - 1) + (2 * NY - 1) + 2 * NY * (NZ - 1))),
        ]


def pieces(lo, hi, group, piece):
    while lo < hi:
        where = lo % group
        count = min(hi - lo, group - where, piece - where % piece)
        yield lo, count, lo // group, where // piece, where % piece
        lo += count


def finish_kernel(scales, actv, ig, g1, g2, actv_out, ig_out, g1out, g2out, sems):
    copies = [pltpu.make_async_copy(ig, ig_out, sems.at[0]), pltpu.make_async_copy(actv, actv_out, sems.at[1])]
    for copy in copies:
        copy.start()
    for row, count, g, k, at_row in pieces(0, 1728, GROUP2, PIECE2):
        got = g2[g // 2, g % 2, k, at_row : at_row + count].astype(F32) * scales[1]
        half = row // 864
        g2out[row % 864 : row % 864 + count, half * 128 : (half + 1) * 128] = got
    for row, count, g, k, at_row in pieces(0, 432, GROUP1, PIECE1):
        g1out[row : row + count] = g1[g, k].astype(F32) * scales[0]
    for copy in copies:
        copy.wait()


def step_kernel(vol_in, w1, w2, cot_in, p0_in, p1_in, p2_in, p3_in, p4_in, actv, ig, g1, g2, *scratch):
    vol, cot, p0, p1, p2, p3, p4, lsem = scratch[35:]
    loads = []
    for k, (src, dst) in enumerate(
        ((vol_in, vol), (p0_in, p0), (p1_in, p1), (cot_in, cot), (p2_in, p2), (p3_in, p3), (p4_in, p4))
    ):
        loads.append(pltpu.make_async_copy(src, dst, lsem.at[k]))
        loads[-1].start()
    xe, xhalo, partial, w1g, w1p, wb, w2g, hid, hhalo, slope, l2, d2, d2e, d1e, un = scratch[:15]
    wsem, hsem = scratch[15:17]
    s1, *bufs1, sems1 = scratch[17:24]
    s2, *bufs2, sems2 = scratch[24:35]
    bufs1.append(g1)
    bufs2.append(g2)
    at = xl, core, y, z, xh = place()
    s, d = lax.axis_index("space"), lax.axis_index("dp")
    n = 2 * NY * NZ
    bottom, top = s == 0, s == n - 1
    upper = {"space": (s + 1) % n}
    lower = {"space": (s + n - 1) % n}
    peers = {"core": device(xl, 1 - core, y, z, xh)}
    for k in range(NY):
        for h in range(2):
            for v in range(2):
                if (k, h, v) != (0, 0, 0):
                    there = xl + h - 2 * xl * h, core, (y + k) % NY, z, xh + v - 2 * xh * v
                    peers["plane", k, h, v] = device(*there)
    for k in range(1, NZ):
        peers["z", k] = device(xl, core, y, (z + k) % NZ, xh)
    peers["upper"], peers["lower"] = upper, lower

    held = []
    for k, (src, dst, size) in enumerate(((w1, w1g, 432), (w2, w2g, 864))):
        at_rows = pl.ds(pl.multiple_of(d * size, 16), size)
        held.append(pltpu.make_async_copy(src, dst.at[at_rows], lsem.at[7 + k]))
        held[-1].start()

    barrier = pltpu.get_barrier_semaphore()
    for peer in peers.values():
        pl.semaphore_signal(barrier, inc=1, device_id=peer, device_id_type=MESH)
    pl.semaphore_wait(barrier, len(peers))

    def rows(q, size, lo, hi):
        return pl.ds(pl.multiple_of(q * size + lo, 16), hi - lo)

    def weight(source, whole, size, cuts, base):
        chunks, slot = [], base
        middle = len(cuts) // 2
        for k in range(middle):
            chunk = []
            for j, peer in ((k, peers["plane", 0, 1, 0]), (middle + k, peers["plane", 0, 1, 1])):
                lo, hi = cuts[j], cuts[j + 1]
                part = source.at[pl.ds(lo, hi - lo)]
                chunk.append((lo, hi, remote(part, whole.at[rows(d, size, lo, hi)], wsem, slot, peer), slot + 1))
                slot += 2
            chunks.append(chunk)
        to_core = remote(source, whole.at[rows(d, size, 0, size)], wsem, slot, peers["core"])
        sent.extend([c[2] for chunk in chunks for c in chunk] + [to_core])
        return chunks, to_core

    sent, passed = [], []
    theirs = (1 - xl) * 2 + core
    chunks1, to_core1 = weight(w1, w1g, 432, (0, 224, 432), 0)
    chunks2, to_core2 = weight(w2, w2g, 864, (0, 224, 432, 656, 864), 5)

    def pass_on(whole, size, chunk):
        for lo, hi, copy, slot in chunk:
            copy.wait_recv()
            part = whole.at[rows(theirs, size, lo, hi)]
            passed.append(remote(part, part, wsem, slot, peers["core"]))

    xe[:, :, 0] = jnp.zeros((9, 3, 16, 128), BF)
    for copy in loads + held:
        copy.wait()

    @pl.loop(0, 8)
    def _(c):
        got = dot(p0[...], vol[:, pl.ds(pl.multiple_of(c * 256, 256), 256)]).astype(BF)
        for i in range(8):
            for e in range(3):
                for u in range(2):
                    xe[i + 1, e, 2 * c + 1 + u] = got[(i * 3 + e) * 16 : (i * 3 + e + 1) * 16, u * 128 : (u + 1) * 128]

    pass_on(w1g, 432, chunks1[0])
    for copy in [to_core1] + passed:
        copy.wait_recv()
    for t in range(9):
        w1p[t * 256 : t * 256 + 64] = jnp.zeros((64, 128), BF)
        w1p[t * 256 + 64 : t * 256 + 256] = w1g[t * 192 : (t + 1) * 192]

    def pairs(plane, taps):
        tiles = []
        for a in taps:
            for e in range(3):
                tiles.append(xe[plane + a, e, 0:16].reshape(256, 128))
                tiles.append(xe[plane + a, e, 1:17].reshape(256, 128))
        return jnp.concatenate(tiles, axis=1)

    def finish_first(o, linear):
        value, gate = act_and_slope(linear)
        hid[o] = value.astype(BF)
        slope[o] = gate.reshape(16, 16, 128)

    partial[...] = dot(pairs(8, (0,)), w1p[0:768]).astype(BF)
    halo_in = remote(partial, xhalo, hsem, 0, upper)
    finish_first(3, dot(pairs(6, range(3)), w1p[...]))
    halo_hid = remote(hid.at[3], hhalo, hsem, 1, upper)
    pass_on(w2g, 864, chunks2[0])

    @pl.loop(1, 3)
    def _(o):
        finish_first(o, dot(pairs(2 * o, range(3)), w1p[...]))

    pass_on(w2g, 864, chunks2[1])
    local_first = dot(pairs(0, (1, 2)), w1p[768:])
    halo_in.wait_recv()
    finish_first(0, local_first + jnp.where(bottom, 0.0, xhalo[...].astype(F32)))

    def place_taps(got, plane):
        for o in range(2):
            a = plane - 2 * o
            if 0 <= a < 3:
                for k in range(9):
                    l2[o * 64 : (o + 1) * 64, (a * 9 + k) * 128 : (a * 9 + k + 1) * 128] = got[k * 64 : (k + 1) * 64]

    for pair in range(2):
        both = jnp.concatenate([hid[2 * pair], hid[2 * pair + 1]], axis=1)
        got = dot(p1[...], both).astype(BF)
        place_taps(got[:, :128], 2 * pair + 1)
        place_taps(got[:, 128:], 2 * pair + 2)
    for t in range(9):
        block = w1p[t * 256 : (t + 1) * 256]
        wb[t * 256 : t * 256 + 128] = block[128:].T
        wb[t * 256 + 128 : (t + 1) * 256] = block[:128].T
    halo_hid.wait_recv()
    rim = jnp.where(bottom, jnp.zeros_like(hhalo), hhalo[...])
    place_taps(dot(p1[...], rim).astype(BF), 0)
    for copy in [to_core2] + passed[2:]:
        copy.wait_recv()

    linear = dot(l2[...], w2g[...])
    value, gate = act_and_slope(linear)
    arriving = jnp.concatenate(
        [cot[o, :, q * 256 : (q + 1) * 256].astype(F32) for o in range(2) for q in range(8)], axis=0
    )
    delta = (arriving * gate).astype(BF)
    d2[0] = delta[:64]
    halo_d2 = remote(d2.at[0], d2.at[2], hsem, 2, lower)
    d2[1] = delta[64:]
    for o in range(2):
        for q in range(8):
            at_row = (o * 8 + q) * 8
            actv[o, :, q * 256 : (q + 1) * 256] = value[at_row : at_row + 8].astype(BF)

    for t in range(27):
        got = dot(l2[:, t * 128 : (t + 1) * 128], delta, 0, 0)
        for q in range(4):
            lo, hi = max(t * 128, q * 864), min(t * 128 + 128, q * 864 + 864)
            for row, count, g, k, at_row in pieces(lo - q * 864, hi - q * 864, GROUP2, PIECE2):
                row += q * 864 - t * 128
                for half in range(2):
                    block = got[row : row + count, half * 128 : (half + 1) * 128].astype(BF)
                    h = half * NY + g
                    s2[q, h // 2, h % 2, k, at_row : at_row + count] = block
    sum2 = Reduction(s2, bufs2, sems2, peers)
    sum1 = LineReduction(s1, bufs1, sems1, peers)
    sum2.cores()

    def spread_delta(o):
        got = dot(p2[...], d2[o]).astype(BF)
        for v in range(4):
            d2e[o, v] = got[v * 64 : (v + 1) * 64]

    taps_of = (((1, 0),), ((2, 0), (0, 1)))

    def hidden_delta(pi):
        for pq in range(2):
            halves = []
            for pj in range(2):
                left, right = [], []
                for a, sa in taps_of[pi]:
                    for e, se in taps_of[pj]:
                        for f, sf in taps_of[pq]:
                            left.append(d2e[sa : sa + 2, sf * 2 + se].reshape(128, 256))
                            t = a * 9 + e * 3 + f
                            right.append(w2g[t * 128 : (t + 1) * 128])
                got = dot(jnp.concatenate(left, axis=1), jnp.concatenate(right, axis=1), 1, 1)
                halves.append(got.reshape(2, 8, 8, 128))
            both = jnp.concatenate(halves, axis=2)
            for i in range(2):
                for q in range(8):
                    d1e[2 * i + pi, 0, 2 * q + pq] = (both[i, q] * slope[2 * i + pi, 2 * q + pq]).astype(BF)

    spread_delta(0)
    spread_delta(1)
    d1e[:, :, 16] = jnp.zeros((5, 2, 16, 128), BF)
    hidden_delta(0)
    halo_d1 = remote(d1e.at[0, 0, pl.ds(0, 16)], d1e.at[4, 0, pl.ds(0, 16)], hsem, 3, lower)
    sum2.plane()
    halo_d2.wait_recv()
    d2[2] = jnp.where(top, jnp.zeros((64, 256), BF), d2[2])
    spread_delta(2)
    hidden_delta(1)

    def first_gradient(start, stop, shift):
        right = jnp.concatenate([d1e[o + shift, 0, 0:16].reshape(256, 128) for o in range(4)], axis=0)

        @pl.loop(start, stop)
        def _(t):
            a, e = t // 3, t % 3
            left = []
            for o in range(4):
                plane = 2 * (o + shift) + a
                left.append(
                    jnp.concatenate(
                        [xe[plane, e, 0:16].reshape(256, 128), xe[plane, e, 1:17].reshape(256, 128)], axis=1
                    )
                )
            got = dot(jnp.concatenate(left, axis=0), right, 0, 0)
            for k in range(24):
                block = t * 24 + k
                g = block % 54 // 7
                s1[block // 54, g, block % 54 % 7] = got[64 + k * 8 : 64 + (k + 1) * 8].astype(BF)

    first_gradient(3, 9, 0)
    halo_d1.wait_recv()
    d1e[4, 0, 0:16] = jnp.where(top, jnp.zeros((16, 16, 128), BF), d1e[4, 0, 0:16])
    first_gradient(0, 3, 1)
    sum1.cores()

    def shift_delta(first, count):
        both = jnp.concatenate([d1e[first + k, 0, 0:16].reshape(256, 128) for k in range(count)], axis=1)
        got = dot(p3[...], both).astype(BF)
        for k in range(count):
            d1e[first + k, 1, 0:16] = got[:, k * 128 : (k + 1) * 128].reshape(16, 16, 128)

    def input_delta(pi, pj):
        @pl.loop(0, 4)
        def _(i):
            left, right = [], []
            for a, sa in taps_of[pi]:
                for e, se in taps_of[pj]:
                    left.append(d1e[i + sa, se, 0:16].reshape(256, 128))
                    left.append(d1e[i + sa, se, 1:17].reshape(256, 128))
                    t = a * 3 + e
                    right.append(wb[t * 256 : (t + 1) * 256])
            got = dot(jnp.concatenate(left, axis=1), jnp.concatenate(right, axis=0)).astype(BF)
            for q in range(16):
                un[2 * i + pi, pj * 16 : (pj + 1) * 16, q * 128 : (q + 1) * 128] = got[q * 16 : (q + 1) * 16]

    shift_delta(0, 2)
    shift_delta(2, 2)
    input_delta(0, 0)
    sum1.along_z()
    sum2.turn()
    input_delta(0, 1)
    shift_delta(4, 1)


    sum2.along_z()
    sum1.plane()
    sum2.gather_z()
    sum1.gather_plane()
    sum2.gather_plane()
    sum1.gather_z()
    input_delta(1, 0)
    input_delta(1, 1)

    @pl.loop(0, 8)
    def _(c):
        lanes = pl.ds(pl.multiple_of(c * 256, 256), 256)
        ig[:, lanes] = dot(p4[...], un[:, :, lanes].reshape(256, 256)).astype(BF)

    sum2.finish()
    sum1.finish()
    for copy in sent + passed + [halo_in, halo_hid, halo_d2, halo_d1]:
        copy.wait_send()
    sum2.drain()
    sum1.drain()


def local(volume, weight_first, weight_second, cotangent):
    cells = 4 * lax.axis_size("space") * 4 * 256
    scales = (float(cells) ** -0.5, float(cells // 8) ** -0.5)
    vmem = pl.BlockSpec(memory_space=pltpu.VMEM)
    anywhere = pl.BlockSpec(memory_space=pl.ANY)
    far = pl.BlockSpec(memory_space=pltpu.HBM)
    shape = jax.ShapeDtypeStruct

    partial = pl.pallas_call(
        step_kernel,
        out_shape=(
            OUT((2, 8, 2048), BF),
            OUT((256, 2048), BF),
            OUT((NZ, 2 * NY, PIECE1, 128), BF),
            OUT((NY, 2, NZ, PIECE2, 128), BF),
        ),
        in_specs=[far] * 9,
        out_specs=(vmem,) * 4,
        scratch_shapes=[
            pltpu.VMEM((9, 3, 17, 16, 128), BF),
            pltpu.VMEM((256, 128), BF),
            pltpu.VMEM((256, 128), BF),
            pltpu.VMEM((1728, 128), BF),
            pltpu.VMEM((2304, 128), BF),
            pltpu.VMEM((2304, 128), BF),
            pltpu.VMEM((3456, 256), BF),
            pltpu.VMEM((4, 256, 128), BF),
            pltpu.VMEM((256, 128), BF),
            pltpu.VMEM((4, 16, 16, 128), F32),
            pltpu.VMEM((128, 3456), BF),
            pltpu.VMEM((3, 64, 256), BF),
            pltpu.VMEM((3, 4, 64, 256), BF),
            pltpu.VMEM((5, 2, 17, 16, 128), BF),
            pltpu.VMEM((8, 32, 2048), BF),
            pltpu.SemaphoreType.DMA((2, 14)),
            pltpu.SemaphoreType.DMA((2, 4)),
        ]
        + LineReduction.scratch(PIECE1)
        + Reduction.scratch(PIECE2)
        + [
            pltpu.VMEM((256, 2048), BF),
            pltpu.VMEM((2, 8, 2048), BF),
            pltpu.VMEM((384, 256), BF),
            pltpu.VMEM((576, 256), BF),
            pltpu.VMEM((256, 64), BF),
            pltpu.VMEM((256, 256), BF),
            pltpu.VMEM((256, 256), BF),
            pltpu.SemaphoreType.DMA((9,)),
        ],
        compiler_params=pltpu.CompilerParams(
            collective_id=0, has_side_effects=True, vmem_limit_bytes=VLIM * 1024 * 1024
        ),
        name="step",
    )(
        *(
            pltpu.with_memory_space_constraint(x, pltpu.HBM)
            for x in (
                volume.reshape(256, 2048),
                weight_first,
                weight_second,
                cotangent.reshape(2, 8, 2048),
                *(jnp.asarray(m) for m in selections()),
            )
        )
    )

    def body(*refs):
        finish_kernel(scales, *refs)

    activations, input_gradient, first, second = pl.pallas_call(
        body,
        out_shape=(
            shape((2, 8, 2048), BF),
            shape((256, 2048), BF),
            shape((432, 128), F32),
            shape((864, 256), F32),
        ),
        in_specs=[vmem] * 4,
        out_specs=(anywhere, anywhere, vmem, vmem),
        scratch_shapes=[pltpu.SemaphoreType.DMA((2,))],
        compiler_params=pltpu.CompilerParams(vmem_limit_bytes=8 * 1024 * 1024),
        name="finish",
    )(*(pltpu.with_memory_space_constraint(x, pltpu.VMEM) for x in partial))
    return (
        activations.reshape(cotangent.shape),
        input_gradient.reshape(volume.shape),
        first,
        second,
    )


def solution(mesh):
    return jax.shard_map(
        local,
        mesh=mesh,
        in_specs=(
            P("dp", "space", None, None),
            P("dp", None),
            P("dp", None),
            P("dp", "space", None, None),
        ),
        out_specs=(
            P("dp", "space", None, None),
            P("dp", "space", None, None),
            P("dp", None),
            P("dp", None),
        ),
        check_vma=False,
    )
```
